32 devices in a mesh: wide: 8 (over z, y), blk: 4 (over x, core).
Axes of the slice: x: 2, y: 2, z: 4, core: 2. Of those that a mesh axis runs over, the one named last changes fastest.
Arguments:
- embeddings: bfloat16 [4096, 768], P(('wide', 'blk')), may hold values from -100 to 100
- bucket_ids: int32 [4096], P(('wide', 'blk')), may hold values from 0 to 7, as said below
- slot_ids: int32 [4096], P(('wide', 'blk')), may hold values from 0 to 31, as said below
- valid_rows: int32 [4096], P(('wide', 'blk')), may hold values 0 or 1
Outputs:
- neighbour_mean: bfloat16 [4096, 768], P(('wide', 'blk'))
- max_cosine: bfloat16 [4096], P(('wide', 'blk'))
The draws below stay inside these ranges and needn't reach their ends.
Inputs may be any that keep to these rules, and one draw needn't show every extreme that they name: `bucket_ids`: bucket of each row. Every bucket holds at most 32 rows of one device; some bucket holds exactly 32 rows of every device. `slot_ids`: no two rows of one device share both bucket and slot.
All inputs are finite; a program needn't handle non-finite values. No bound on the sum of `valid_rows` on one device may be relied on, other than what follows from the above.
Results may differ from the reference program's by a relative error of at most 0.003.
Values may be sent and summed in bfloat16 or wider, within the bound.
A program may use at most 64 MiB of HBM per device.

```python
import jax
import jax.numpy as jnp
from jax import lax

D = 768
ROW_DEV = 128
BUCKETS = 8
SLOTS = 32
ROWS = 4096
N_WIDE = 8
N_BLK = 4


def chosen_cells(key):
    base_key = jax.random.fold_in(key, 7)
    key_parts = jax.random.split(base_key, 5)
    device_count = ROWS // ROW_DEV
    cell_count = BUCKETS * SLOTS
    bucket_of_cell = jnp.arange(cell_count, dtype=jnp.int32) // SLOTS
    popular = jax.random.randint(key_parts[0], (BUCKETS,), 0, 4)
    hot_bucket = jax.random.randint(key_parts[1], (), 0, BUCKETS)
    own_bucket = jax.random.randint(key_parts[2], (device_count, 1), 0, BUCKETS)
    jitter = jax.random.randint(key_parts[3], (device_count, cell_count), 0, 4096)
    forced = (bucket_of_cell[None, :] == hot_bucket) | (bucket_of_cell[None, :] == own_bucket)
    scores = jitter + popular[bucket_of_cell][None, :] * 2048 + forced.astype(jnp.int32) * 16384
    scores = scores * cell_count + jnp.arange(cell_count, dtype=jnp.int32)[None, :]
    picked = lax.top_k(scores, ROW_DEV)[1]
    order_keys = jax.random.randint(key_parts[4], (device_count, ROW_DEV), 0, 65536) * ROW_DEV + jnp.arange(ROW_DEV, dtype=jnp.int32)[None, :]
    order = lax.top_k(order_keys, ROW_DEV)[1]
    return jnp.take_along_axis(picked, order, axis=1).reshape(ROWS).astype(jnp.int32)


def draw_bucket_ids(key, part):
    return (chosen_cells(key) // SLOTS).astype(jnp.int32)


def draw_slot_ids(key, part):
    return (chosen_cells(key) % SLOTS).astype(jnp.int32)


def draw_embeddings(key, part):
    cell_ids = chosen_cells(key)
    bucket_rows = cell_ids // SLOTS
    key_parts = jax.random.split(jax.random.fold_in(key, 13), 4)
    centers = jax.random.truncated_normal(key_parts[0], -4.0, 4.0, (BUCKETS, D), jnp.float32)
    sub_centers = jax.random.truncated_normal(key_parts[1], -4.0, 4.0, (BUCKETS * 16, D), jnp.float32)
    sub_ids = jax.random.randint(key_parts[2], (ROWS,), 0, 16)
    noise = jax.random.truncated_normal(key_parts[3], -4.0, 4.0, (ROWS, D), jnp.float32)
    float_rows = 0.8 * centers[bucket_rows] + sub_centers[bucket_rows * 16 + sub_ids] + 0.7 * noise
    return float_rows.astype(jnp.bfloat16)


def touch_ends(drawn, rng, smallest, top_value):
    index_at = [jax.random.randint(jax.random.fold_in(rng, axis), (), 0, length) for axis, length in enumerate(drawn.shape)]
    longest = drawn.shape.index(max(drawn.shape))
    beside = index_at[:longest] + [(index_at[longest] + 1) % drawn.shape[longest]] + index_at[longest + 1:]
    return drawn.at[tuple(index_at)].set(smallest).at[tuple(beside)].set(top_value)


def setup_inputs(seed: int = 0) -> dict:
    key_list = jax.random.split(jax.random.key(seed), 5)
    embeddings = draw_embeddings(jax.random.fold_in(key_list[4], 71), 0)
    bucket_ids = draw_bucket_ids(jax.random.fold_in(key_list[4], 71), 0)
    slot_ids = draw_slot_ids(jax.random.fold_in(key_list[4], 71), 0)
    valid_rows = touch_ends((jax.random.randint(key_list[3], (ROWS,), 0, 8) < 7).astype(jnp.int32), jax.random.fold_in(key_list[3], 1), 0, 1)
    return dict(embeddings=embeddings, bucket_ids=bucket_ids, slot_ids=slot_ids, valid_rows=valid_rows)


sharpness = 10.0

def unit_rows(embeddings):
    float_rows = embeddings.astype(jnp.float32)
    inverse_norm = lax.rsqrt(lax.optimization_barrier(jnp.mean(float_rows * float_rows, axis=1, keepdims=True)) + 1e-06)
    return (float_rows * inverse_norm).astype(jnp.bfloat16)

def bucket_stats(queries, query_pos, key_rows, key_flags, key_pos):
    feature_count = queries.shape[1]
    cosine = lax.dot_general(queries, key_rows, (((1,), (1,)), ((), ())), preferred_element_type=jnp.float32) / feature_count
    usable = (key_flags[None, :] > 0) & (query_pos[:, None] != key_pos[None, :])
    best_cos = lax.optimization_barrier(jnp.max(jnp.where(usable, cosine, -1.0), axis=1))
    weights = jnp.where(usable, jnp.exp(sharpness * (cosine - 1.0)), 0.0)
    weight_total = lax.optimization_barrier(jnp.sum(weights, axis=1))
    summed = jnp.dot(weights.astype(jnp.bfloat16), key_rows, preferred_element_type=jnp.float32)
    return (best_cos, weight_total, summed)

def reference(embeddings, bucket_ids, slot_ids, valid_rows):
    unit_vectors = unit_rows(embeddings)
    row_index = jnp.arange(ROWS, dtype=jnp.int32)
    device = row_index // ROW_DEV
    source = device // N_BLK
    block_index = device % N_BLK
    per_bucket = N_BLK * N_WIDE * SLOTS
    position = (bucket_ids * per_bucket + (block_index * N_WIDE + source) * SLOTS + slot_ids).astype(jnp.int32)
    bucket_grid = jnp.zeros((BUCKETS * per_bucket, D), jnp.bfloat16).at[position].set(unit_vectors)
    bucket_flags = jnp.zeros((BUCKETS * per_bucket,), jnp.bfloat16).at[position].set(valid_rows.astype(jnp.bfloat16))
    bucket_grid = bucket_grid.reshape(BUCKETS, per_bucket, D)
    bucket_flags = bucket_flags.reshape(BUCKETS, per_bucket)

    def one_bucket(bucket_pair):
        member_rows, member_flags = bucket_pair
        positions = jnp.arange(per_bucket, dtype=jnp.int32)
        best_cos, weight_total, summed = bucket_stats(member_rows, positions, member_rows, member_flags, positions)
        mean_rows = ((member_rows.astype(jnp.float32) + summed) / (1.0 + weight_total[:, None])).astype(jnp.bfloat16)
        return (mean_rows, best_cos.astype(jnp.bfloat16))
    mean_grid, best_grid = lax.map(one_bucket, (bucket_grid, bucket_flags))
    neighbour_mean = mean_grid.reshape(BUCKETS * per_bucket, D)[position]
    max_cosine = best_grid.reshape(BUCKETS * per_bucket)[position]
    return (neighbour_mean, max_cosine)
```

```python
import functools

import jax
import jax.numpy as jnp
from jax import lax
from jax.experimental import pallas as pl
from jax.experimental.pallas import tpu as pltpu
from jax.sharding import PartitionSpec as P

sharpness = 10.0


def from_behind(value, axis, steps):
    count = lax.axis_size(axis)
    pairs = [(source, (source + steps) % count) for source in range(count)]
    return lax.ppermute(value, axis, pairs)


def unit_rows(embeddings):
    float_rows = embeddings.astype(jnp.float32)
    inverse_norm = lax.rsqrt(jnp.mean(float_rows * float_rows, axis=1, keepdims=True) + 1e-06)
    return (float_rows * inverse_norm).astype(jnp.bfloat16)


def bucket_stats(queries, query_pos, key_rows, key_flags, key_pos):
    feature_count = queries.shape[1]
    cosine = (
        lax.dot_general(
            queries, key_rows, (((1,), (1,)), ((), ())), preferred_element_type=jnp.float32
        )
        / feature_count
    )
    usable = (key_flags[None, :] > 0) & (query_pos[:, None] != key_pos[None, :])
    best_cos = jnp.max(jnp.where(usable, cosine, -1.0), axis=1)
    weights = jnp.where(usable, jnp.exp(sharpness * (cosine - 1.0)), 0.0)
    weight_total = jnp.sum(weights, axis=1)
    summed = jnp.dot(weights.astype(jnp.bfloat16), key_rows, preferred_element_type=jnp.float32)
    return (best_cos, weight_total, summed)


def by_bucket(embeddings, bucket_ids, slot_ids, valid_rows):
    unit_vectors = unit_rows(embeddings)
    row_count, feature_count = unit_vectors.shape
    groups = lax.axis_size("wide")
    blocks = lax.axis_size("blk")
    slot_count = 2 * row_count // groups
    block_rows = groups * slot_count
    cell_ids = bucket_ids * slot_count + slot_ids
    outgoing = jnp.zeros((block_rows, feature_count), jnp.bfloat16).at[cell_ids].set(unit_vectors)
    flag_rows = (
        jnp.zeros((block_rows,), jnp.bfloat16).at[cell_ids].set(valid_rows.astype(jnp.bfloat16))
    )
    arrived, arrived_flags = (
        lax.all_to_all(
            outgoing.reshape(groups, slot_count, feature_count),
            "wide",
            split_axis=0,
            concat_axis=0,
            tiled=True,
        ),
        lax.all_to_all(
            flag_rows.reshape(groups, slot_count), "wide", split_axis=0, concat_axis=0, tiled=True
        ),
    )
    queries = arrived.reshape(block_rows, feature_count)
    query_flags = arrived_flags.reshape(block_rows)
    my_block = lax.axis_index("blk")
    query_pos = my_block * block_rows + jnp.arange(block_rows, dtype=jnp.int32)

    def absorb(running, key_rows, key_flags, key_start):
        key_pos = key_start + jnp.arange(key_rows.shape[0], dtype=jnp.int32)
        best_cos, weight_total, summed = bucket_stats(
            queries, query_pos, key_rows, key_flags, key_pos
        )
        return (jnp.maximum(running[0], best_cos), running[1] + weight_total, running[2] + summed)

    initial = (
        jnp.full((block_rows,), -1.0, jnp.float32),
        jnp.zeros((block_rows,), jnp.float32),
        jnp.zeros((block_rows, feature_count), jnp.float32),
    )
    key_rows, key_flags = (queries, query_flags)
    running = absorb(initial, key_rows, key_flags, my_block * block_rows)
    for turn_index in range(1, blocks):
        key_rows, key_flags = from_behind((key_rows, key_flags), "blk", 1)
        running = absorb(
            running, key_rows, key_flags, (my_block - turn_index) % blocks * block_rows
        )
    best_cos, weight_total, summed = running
    mean_rows = ((queries.astype(jnp.float32) + summed) / (1.0 + weight_total[:, None])).astype(
        jnp.bfloat16
    )
    back_mean, back_best = (
        lax.all_to_all(
            mean_rows.reshape(groups, slot_count, feature_count),
            "wide",
            split_axis=0,
            concat_axis=0,
            tiled=True,
        ),
        lax.all_to_all(
            best_cos.astype(jnp.bfloat16).reshape(groups, slot_count),
            "wide",
            split_axis=0,
            concat_axis=0,
            tiled=True,
        ),
    )
    neighbour_mean = back_mean.reshape(block_rows, feature_count)[cell_ids]
    max_cosine = back_best.reshape(block_rows)[cell_ids]
    return (neighbour_mean, max_cosine)


PAIR = 2
PIECES = 2


def arrival_order(place, count):
    low, high = place, count - 1 - place
    order = []
    for distance in range(1, count):
        if distance <= low:
            order.append(place - distance)
        if distance <= high:
            order.append(place + distance)
    return order


def dense_kernel(
    planes, emb_ref, bucket_ref, valid_ref, mean_ref, best_ref,
    keys, key_meta, queries, query_meta, query_col, total, peak, weight,
    part_out, part_in, stat_out, stat_in,
    z_send, z_recv, zm_send, zm_recv, c_send, c_recv, cm_send, cm_recv,
    q_send, q_recv, qm_send, qm_recv, p_send, p_recv, s_send, s_recv,
):
    rows, features = emb_ref.shape
    spots = queries.shape[0]
    wide, blk = lax.axis_index("wide"), lax.axis_index("blk")
    z, y = lax.div(wide, PAIR), lax.rem(wide, PAIR)
    x, core = lax.div(blk, PAIR), lax.rem(blk, PAIR)
    other = 1 - core
    columns = spots // PAIR
    piece = rows // PIECES

    def at(z_at, y_at, x_at, core_at):
        return (z_at * PAIR + y_at, x_at * PAIR + core_at)

    def spot_device(spot):
        dy, dx = divmod(spot, columns)
        return at(z, lax.rem(y + dy, PAIR), lax.rem(x + dx, columns), core)

    def seen_from(spot):
        dy, dx = divmod(spot, columns)
        return (-dy) % PAIR * columns + (-dx) % columns

    def remote(source, target, send, recv, device):
        return pltpu.make_async_remote_copy(
            src_ref=source, dst_ref=target, send_sem=send, recv_sem=recv,
            device_id=device, device_id_type=pl.DeviceIdType.MESH,
        )

    partner = at(z, y, x, other)
    has_low, has_high = z > 0, z < planes - 1

    barrier = pltpu.get_barrier_semaphore()

    def greet(device):
        pl.semaphore_signal(barrier, inc=1, device_id=device, device_id_type=pl.DeviceIdType.MESH)

    greet(partner)
    for spot in range(1, spots):
        greet(spot_device(spot))

    @pl.when(has_low)
    def _():
        greet(at(z - 1, y, x, core))

    @pl.when(has_high)
    def _():
        greet(at(z + 1, y, x, core))

    floats = emb_ref[...].astype(jnp.float32)
    inverse = lax.rsqrt(jnp.mean(floats * floats, axis=1, keepdims=True) + 1e-06)
    unit = (floats * inverse).astype(jnp.bfloat16)
    keys[z, core] = unit
    queries[0] = unit
    meta = jnp.concatenate([bucket_ref[...], valid_ref[...]], axis=0).astype(jnp.float32)
    key_meta[z, core] = meta
    query_meta[0] = meta

    pl.semaphore_wait(barrier, jnp.where(has_low & has_high, spots + 2, spots + 1))

    def z_meta(source, way, to):
        ref = key_meta.at[source, core]
        return remote(
            ref, ref, zm_send.at[source, way], zm_recv.at[source], at(to, y, x, core)
        )

    def z_copy(source, way, to, part):
        ref = keys.at[source, core, pl.ds(part * piece, piece)]
        return remote(
            ref, ref, z_send.at[source, way, part], z_recv.at[source, part], at(to, y, x, core)
        )

    def c_meta(source, side):
        ref = key_meta.at[source, side]
        return remote(ref, ref, cm_send.at[source], cm_recv.at[source], partner)

    def c_copy(source, side, part):
        ref = keys.at[source, side, pl.ds(part * piece, piece)]
        return remote(ref, ref, c_send.at[source, part], c_recv.at[source, part], partner)

    def q_meta(spot):
        mine = seen_from(spot)
        return remote(
            query_meta.at[0], query_meta.at[mine], qm_send.at[spot], qm_recv.at[mine],
            spot_device(spot),
        )

    def q_copy(spot):
        mine = seen_from(spot)
        return remote(
            queries.at[0], queries.at[mine], q_send.at[spot], q_recv.at[mine], spot_device(spot)
        )

    def send_ways(source, act):
        @pl.when((source <= z) & has_high)
        def _():
            act(1, z + 1)

        @pl.when((source >= z) & has_low)
        def _():
            act(0, z - 1)

    send_ways(z, lambda way, to: z_meta(z, way, to).start())
    for part in range(PIECES):
        send_ways(z, lambda way, to: z_copy(z, way, to, part).start())
    c_meta(z, core).start()
    for part in range(PIECES):
        c_copy(z, core, part).start()
    for spot in range(spots - 1, 0, -1):
        q_meta(spot).start()
        q_copy(spot).start()

    def column_of(spot):
        row = query_meta[spot, 0:1, :]
        query_col[spot] = jnp.transpose(jnp.broadcast_to(row, (rows, rows)))

    def absorb(first, last, source, fresh):
        count = (last - first) * rows
        chosen = queries[first:last].reshape(count, features)
        block = keys[source].reshape(PAIR * rows, features)
        cosine = lax.dot_general(
            chosen, block, (((1,), (1,)), ((), ())), preferred_element_type=jnp.float32
        ) * (1.0 / features)
        buckets = query_col[first:last].reshape(count, rows)
        line = lax.broadcasted_iota(jnp.int32, (count, rows), 0)
        lane = lax.broadcasted_iota(jnp.int32, (count, rows), 1)
        factors = []
        peaks = None
        sums = None
        for side in range(PAIR):
            key_bucket = key_meta[source, side, 0:1, :]
            key_flag = key_meta[source, side, 1:2, :]
            wanted = jnp.where(key_flag > 0, key_bucket, -1.0)
            usable = buckets == wanted
            if first == 0:
                own = (source == z) & (core == side)
                shift = jnp.where(own, 0, count + rows)
                usable = usable & (line + shift != lane)
            values = cosine[:, side * rows : (side + 1) * rows]
            best = jnp.where(usable, values, -1.0)
            factor = jnp.where(usable, jnp.exp(sharpness * (values - 1.0)), 0.0)
            factors.append(factor.astype(jnp.bfloat16))
            peaks = best if peaks is None else jnp.maximum(peaks, best)
            sums = factor if sums is None else sums + factor
        summed = jnp.dot(
            jnp.concatenate(factors, axis=1), block, preferred_element_type=jnp.float32
        )
        part = (last - first, rows)
        if fresh:
            peak[first:last] = peaks.reshape(*part, rows)
            weight[first:last] = sums.reshape(*part, rows)
            total[first:last] = summed.reshape(*part, features)
        else:
            peak[first:last] = jnp.maximum(peak[first:last], peaks.reshape(*part, rows))
            weight[first:last] += sums.reshape(*part, rows)
            total[first:last] += summed.reshape(*part, features)

    def wait_partner(source):
        c_meta(source, other).wait_recv()
        for part in range(PIECES):
            c_copy(source, other, part).wait_recv()

    def take(source):
        z_meta(source, 0, z).wait_recv()
        send_ways(source, lambda way, to: z_meta(source, way, to).start())
        c_meta(source, core).start()
        for part in range(PIECES):
            z_copy(source, 0, z, part).wait_recv()
            send_ways(source, lambda way, to: z_copy(source, way, to, part).start())
            c_copy(source, core, part).start()

    orders = [arrival_order(place, planes) for place in range(planes)]

    def source_at(turn):
        source = jnp.int32(orders[0][turn])
        for place in range(1, planes):
            source = jnp.where(z == place, orders[place][turn], source)
        return source

    sources = [source_at(turn) for turn in range(planes - 1)]
    inner = has_low & has_high

    column_of(0)
    wait_partner(z)
    absorb(0, 1, z, True)
    for source in sources[:-1]:
        take(source)
        wait_partner(source)
        absorb(0, 1, source, False)
    final = sources[-1]

    @pl.when(inner)
    def _():
        take(final)

    for spot in range(1, spots):
        q_meta(seen_from(spot)).wait_recv()
        column_of(spot)
        q_copy(seen_from(spot)).wait_recv()
    absorb(1, spots, z, True)
    for source in sources[:-1]:
        absorb(1, spots, source, False)

    @pl.when(jnp.logical_not(inner))
    def _():
        take(final)

    wait_partner(final)
    absorb(0, spots, final, False)

    def stat_rows(spot):
        top = jnp.max(jnp.transpose(peak[spot]), axis=0, keepdims=True)
        mass = jnp.sum(jnp.transpose(weight[spot]), axis=0, keepdims=True)
        return top, mass

    def p_copy(spot):
        mine = seen_from(spot)
        return remote(
            part_out.at[spot], part_in.at[mine], p_send.at[spot], p_recv.at[mine],
            spot_device(spot),
        )

    def s_copy(spot):
        mine = seen_from(spot)
        return remote(
            stat_out.at[spot], stat_in.at[mine], s_send.at[spot], s_recv.at[mine],
            spot_device(spot),
        )

    for spot in range(spots - 1, 0, -1):
        part_out[spot] = total[spot].astype(jnp.bfloat16)
        p_copy(spot).start()
    for spot in range(spots - 1, 0, -1):
        stat_out[spot] = jnp.concatenate(stat_rows(spot), axis=0)
        s_copy(spot).start()

    top, mass = stat_rows(0)
    result = total[0] + queries[0].astype(jnp.float32)
    for spot in range(1, spots):
        s_copy(seen_from(spot)).wait_recv()
        top = jnp.maximum(top, stat_in[spot, 0:1, :])
        mass = mass + stat_in[spot, 1:2, :]
    best_ref[...] = top.astype(jnp.bfloat16)
    below = jnp.transpose(jnp.broadcast_to(1.0 + mass, (rows, rows)))[:, 0:1]
    for spot in range(1, spots):
        p_copy(seen_from(spot)).wait_recv()
        result = result + part_in[spot].astype(jnp.float32)
    mean_ref[...] = (result / below).astype(jnp.bfloat16)

    send_ways(z, lambda way, to: z_meta(z, way, to).wait_send())
    for part in range(PIECES):
        send_ways(z, lambda way, to: z_copy(z, way, to, part).wait_send())
    c_meta(z, core).wait_send()
    for part in range(PIECES):
        c_copy(z, core, part).wait_send()
    for source in sources:
        send_ways(source, lambda way, to: z_meta(source, way, to).wait_send())
        c_meta(source, core).wait_send()
        for part in range(PIECES):
            send_ways(source, lambda way, to: z_copy(source, way, to, part).wait_send())
            c_copy(source, core, part).wait_send()
    for spot in range(1, spots):
        q_meta(spot).wait_send()
        q_copy(spot).wait_send()
        p_copy(spot).wait_send()
        s_copy(spot).wait_send()


def dense(embeddings, bucket_ids, valid_rows):
    rows, features = embeddings.shape
    planes = lax.axis_size("wide") // PAIR
    spots = lax.axis_size("blk")
    dma = pltpu.SemaphoreType.DMA
    vmem = pl.BlockSpec(memory_space=pltpu.VMEM)
    mean, best = pl.pallas_call(
        functools.partial(dense_kernel, planes),
        out_shape=(
            jax.ShapeDtypeStruct((rows, features), jnp.bfloat16),
            jax.ShapeDtypeStruct((1, rows), jnp.bfloat16),
        ),
        in_specs=[vmem] * 3,
        out_specs=(vmem, vmem),
        scratch_shapes=[
            pltpu.VMEM((planes, PAIR, rows, features), jnp.bfloat16),
            pltpu.VMEM((planes, PAIR, 2, rows), jnp.float32),
            pltpu.VMEM((spots, rows, features), jnp.bfloat16),
            pltpu.VMEM((spots, 2, rows), jnp.float32),
            pltpu.VMEM((spots, rows, rows), jnp.float32),
            pltpu.VMEM((spots, rows, features), jnp.float32),
            pltpu.VMEM((spots, rows, rows), jnp.float32),
            pltpu.VMEM((spots, rows, rows), jnp.float32),
            pltpu.VMEM((spots, rows, features), jnp.bfloat16),
            pltpu.VMEM((spots, rows, features), jnp.bfloat16),
            pltpu.VMEM((spots, 2, rows), jnp.float32),
            pltpu.VMEM((spots, 2, rows), jnp.float32),
            dma((planes, 2, PIECES)), dma((planes, PIECES)), dma((planes, 2)), dma((planes,)),
            dma((planes, PIECES)), dma((planes, PIECES)), dma((planes,)), dma((planes,)),
            dma((spots,)), dma((spots,)), dma((spots,)), dma((spots,)),
            dma((spots,)), dma((spots,)), dma((spots,)), dma((spots,)),
        ],
        compiler_params=pltpu.CompilerParams(
            collective_id=0, has_side_effects=True, vmem_limit_bytes=56 * 1024 * 1024
        ),
    )(embeddings, bucket_ids.reshape(1, rows), valid_rows.reshape(1, rows))
    return mean, best.reshape(rows)


def on_device(embeddings, bucket_ids, slot_ids, valid_rows):
    rows = embeddings.shape[0]
    groups = lax.axis_size("wide")
    blocks = lax.axis_size("blk")
    bucket_work = blocks * (2 * rows) ** 2
    dense_work = groups * blocks * rows**2
    fits = groups % PAIR == 0 and groups > PAIR and blocks == PAIR * PAIR and rows == 128
    if fits and dense_work <= 4 * bucket_work:
        return dense(embeddings, bucket_ids, valid_rows)
    return by_bucket(embeddings, bucket_ids, slot_ids, valid_rows)


def solution(mesh):
    in_specs = (
        P(("wide", "blk"), None),
        P(("wide", "blk")),
        P(("wide", "blk")),
        P(("wide", "blk")),
    )
    out_specs = (P(("wide", "blk"), None), P(("wide", "blk")))
    return jax.shard_map(
        on_device, mesh=mesh, in_specs=in_specs, out_specs=out_specs, check_vma=False
    )
```

```python
import functools

import jax
import jax.numpy as jnp
from jax import lax
from jax.experimental import pallas as pl
from jax.experimental.pallas import tpu as pltpu
from jax.sharding import PartitionSpec as P

sharpness = 10.0


def from_behind(value, axis, steps):
    count = lax.axis_size(axis)
    pairs = [(source, (source + steps) % count) for source in range(count)]
    return lax.ppermute(value, axis, pairs)


def unit_rows(embeddings):
    float_rows = embeddings.astype(jnp.float32)
    inverse_norm = lax.rsqrt(jnp.mean(float_rows * float_rows, axis=1, keepdims=True) + 1e-06)
    return (float_rows * inverse_norm).astype(jnp.bfloat16)


def bucket_stats(queries, query_pos, key_rows, key_flags, key_pos):
    feature_count = queries.shape[1]
    cosine = (
        lax.dot_general(
            queries, key_rows, (((1,), (1,)), ((), ())), preferred_element_type=jnp.float32
        )
        / feature_count
    )
    usable = (key_flags[None, :] > 0) & (query_pos[:, None] != key_pos[None, :])
    best_cos = jnp.max(jnp.where(usable, cosine, -1.0), axis=1)
    weights = jnp.where(usable, jnp.exp(sharpness * (cosine - 1.0)), 0.0)
    weight_total = jnp.sum(weights, axis=1)
    summed = jnp.dot(weights.astype(jnp.bfloat16), key_rows, preferred_element_type=jnp.float32)
    return (best_cos, weight_total, summed)


def by_bucket(embeddings, bucket_ids, slot_ids, valid_rows):
    unit_vectors = unit_rows(embeddings)
    row_count, feature_count = unit_vectors.shape
    groups = lax.axis_size("wide")
    blocks = lax.axis_size("blk")
    slot_count = 2 * row_count // groups
    block_rows = groups * slot_count
    cell_ids = bucket_ids * slot_count + slot_ids
    outgoing = jnp.zeros((block_rows, feature_count), jnp.bfloat16).at[cell_ids].set(unit_vectors)
    flag_rows = (
        jnp.zeros((block_rows,), jnp.bfloat16).at[cell_ids].set(valid_rows.astype(jnp.bfloat16))
    )
    arrived, arrived_flags = (
        lax.all_to_all(
            outgoing.reshape(groups, slot_count, feature_count),
            "wide",
            split_axis=0,
            concat_axis=0,
            tiled=True,
        ),
        lax.all_to_all(
            flag_rows.reshape(groups, slot_count), "wide", split_axis=0, concat_axis=0, tiled=True
        ),
    )
    queries = arrived.reshape(block_rows, feature_count)
    query_flags = arrived_flags.reshape(block_rows)
    my_block = lax.axis_index("blk")
    query_pos = my_block * block_rows + jnp.arange(block_rows, dtype=jnp.int32)

    def absorb(running, key_rows, key_flags, key_start):
        key_pos = key_start + jnp.arange(key_rows.shape[0], dtype=jnp.int32)
        best_cos, weight_total, summed = bucket_stats(
            queries, query_pos, key_rows, key_flags, key_pos
        )
        return (jnp.maximum(running[0], best_cos), running[1] + weight_total, running[2] + summed)

    initial = (
        jnp.full((block_rows,), -1.0, jnp.float32),
        jnp.zeros((block_rows,), jnp.float32),
        jnp.zeros((block_rows, feature_count), jnp.float32),
    )
    key_rows, key_flags = (queries, query_flags)
    running = absorb(initial, key_rows, key_flags, my_block * block_rows)
    for turn_index in range(1, blocks):
        key_rows, key_flags = from_behind((key_rows, key_flags), "blk", 1)
        running = absorb(
            running, key_rows, key_flags, (my_block - turn_index) % blocks * block_rows
        )
    best_cos, weight_total, summed = running
    mean_rows = ((queries.astype(jnp.float32) + summed) / (1.0 + weight_total[:, None])).astype(
        jnp.bfloat16
    )
    back_mean, back_best = (
        lax.all_to_all(
            mean_rows.reshape(groups, slot_count, feature_count),
            "wide",
            split_axis=0,
            concat_axis=0,
            tiled=True,
        ),
        lax.all_to_all(
            best_cos.astype(jnp.bfloat16).reshape(groups, slot_count),
            "wide",
            split_axis=0,
            concat_axis=0,
            tiled=True,
        ),
    )
    neighbour_mean = back_mean.reshape(block_rows, feature_count)[cell_ids]
    max_cosine = back_best.reshape(block_rows)[cell_ids]
    return (neighbour_mean, max_cosine)


PAIR = 2
PIECES = 4


def arrival_order(place, count):
    low, high = place, count - 1 - place
    order = []
    for distance in range(1, count):
        if distance <= low:
            order.append(place - distance)
        if distance <= high:
            order.append(place + distance)
    return order


def dense_kernel(
    planes, emb_ref, bucket_ref, valid_ref, mean_ref, best_ref,
    keys, key_meta, queries, query_meta, query_col, total, peak, weight,
    part_out, part_in, stat_out, stat_in,
    z_send, z_recv, zm_send, zm_recv, c_send, c_recv, cm_send, cm_recv,
    q_send, q_recv, qm_send, qm_recv, p_send, p_recv, s_send, s_recv,
):
    rows, features = emb_ref.shape
    spots = queries.shape[0]
    wide, blk = lax.axis_index("wide"), lax.axis_index("blk")
    z, y = lax.div(wide, PAIR), lax.rem(wide, PAIR)
    x, core = lax.div(blk, PAIR), lax.rem(blk, PAIR)
    other = 1 - core
    columns = spots // PAIR
    piece = rows // PIECES

    def at(z_at, y_at, x_at, core_at):
        return (z_at * PAIR + y_at, x_at * PAIR + core_at)

    def spot_device(spot):
        dy, dx = divmod(spot, columns)
        return at(z, lax.rem(y + dy, PAIR), lax.rem(x + dx, columns), core)

    def seen_from(spot):
        dy, dx = divmod(spot, columns)
        return (-dy) % PAIR * columns + (-dx) % columns

    def remote(source, target, send, recv, device):
        return pltpu.make_async_remote_copy(
            src_ref=source, dst_ref=target, send_sem=send, recv_sem=recv,
            device_id=device, device_id_type=pl.DeviceIdType.MESH,
        )

    partner = at(z, y, x, other)
    has_low, has_high = z > 0, z < planes - 1

    barrier = pltpu.get_barrier_semaphore()

    def greet(device):
        pl.semaphore_signal(barrier, inc=1, device_id=device, device_id_type=pl.DeviceIdType.MESH)

    greet(partner)
    for spot in range(1, spots):
        greet(spot_device(spot))

    @pl.when(has_low)
    def _():
        greet(at(z - 1, y, x, core))

    @pl.when(has_high)
    def _():
        greet(at(z + 1, y, x, core))

    floats = emb_ref[...].astype(jnp.float32)
    inverse = lax.rsqrt(jnp.mean(floats * floats, axis=1, keepdims=True) + 1e-06)
    unit = (floats * inverse).astype(jnp.bfloat16)
    keys[z, core] = unit
    queries[0] = unit
    meta = jnp.concatenate([bucket_ref[...], valid_ref[...]], axis=0).astype(jnp.float32)
    key_meta[z, core] = meta
    query_meta[0] = meta

    pl.semaphore_wait(barrier, jnp.where(has_low & has_high, spots + 2, spots + 1))

    def z_meta(source, way, to):
        ref = key_meta.at[source, core]
        return remote(
            ref, ref, zm_send.at[source, way], zm_recv.at[source], at(to, y, x, core)
        )

    def z_copy(source, way, to, part):
        ref = keys.at[source, core, pl.ds(part * piece, piece)]
        return remote(
            ref, ref, z_send.at[source, way, part], z_recv.at[source, part], at(to, y, x, core)
        )

    def c_meta(source, side):
        ref = key_meta.at[source, side]
        return remote(ref, ref, cm_send.at[source], cm_recv.at[source], partner)

    def c_copy(source, side, part):
        ref = keys.at[source, side, pl.ds(part * piece, piece)]
        return remote(ref, ref, c_send.at[source, part], c_recv.at[source, part], partner)

    def q_meta(spot):
        mine = seen_from(spot)
        return remote(
            query_meta.at[0], query_meta.at[mine], qm_send.at[spot], qm_recv.at[mine],
            spot_device(spot),
        )

    def q_copy(spot):
        mine = seen_from(spot)
        return remote(
            queries.at[0], queries.at[mine], q_send.at[spot], q_recv.at[mine], spot_device(spot)
        )

    def send_ways(source, act):
        @pl.when((source <= z) & has_high)
        def _():
            act(1, z + 1)

        @pl.when((source >= z) & has_low)
        def _():
            act(0, z - 1)

    send_ways(z, lambda way, to: z_meta(z, way, to).start())
    for part in range(PIECES):
        send_ways(z, lambda way, to: z_copy(z, way, to, part).start())
    c_meta(z, core).start()
    for part in range(PIECES):
        c_copy(z, core, part).start()
    for spot in range(spots - 1, 0, -1):
        q_meta(spot).start()
        q_copy(spot).start()

    def column_of(spot):
        row = query_meta[spot, 0:1, :]
        query_col[spot] = jnp.transpose(jnp.broadcast_to(row, (rows, rows)))

    def absorb(first, last, source, fresh):
        count = (last - first) * rows
        chosen = queries[first:last].reshape(count, features)
        block = keys[source].reshape(PAIR * rows, features)
        cosine = lax.dot_general(
            chosen, block, (((1,), (1,)), ((), ())), preferred_element_type=jnp.float32
        ) * (1.0 / features)
        buckets = query_col[first:last].reshape(count, rows)
        line = lax.broadcasted_iota(jnp.int32, (count, rows), 0)
        lane = lax.broadcasted_iota(jnp.int32, (count, rows), 1)
        factors = []
        peaks = None
        sums = None
        for side in range(PAIR):
            key_bucket = key_meta[source, side, 0:1, :]
            key_flag = key_meta[source, side, 1:2, :]
            wanted = jnp.where(key_flag > 0, key_bucket, -1.0)
            usable = buckets == wanted
            if first == 0:
                own = (source == z) & (core == side)
                shift = jnp.where(own, 0, count + rows)
                usable = usable & (line + shift != lane)
            values = cosine[:, side * rows : (side + 1) * rows]
            best = jnp.where(usable, values, -1.0)
            factor = jnp.where(usable, jnp.exp(sharpness * (values - 1.0)), 0.0)
            factors.append(factor.astype(jnp.bfloat16))
            peaks = best if peaks is None else jnp.maximum(peaks, best)
            sums = factor if sums is None else sums + factor
        summed = jnp.dot(
            jnp.concatenate(factors, axis=1), block, preferred_element_type=jnp.float32
        )
        part = (last - first, rows)
        if fresh:
            peak[first:last] = peaks.reshape(*part, rows)
            weight[first:last] = sums.reshape(*part, rows)
            total[first:last] = summed.reshape(*part, features)
        else:
            peak[first:last] = jnp.maximum(peak[first:last], peaks.reshape(*part, rows))
            weight[first:last] += sums.reshape(*part, rows)
            total[first:last] += summed.reshape(*part, features)

    def wait_partner(source):
        c_meta(source, other).wait_recv()
        for part in range(PIECES):
            c_copy(source, other, part).wait_recv()

    def take(*arriving):
        for source in arriving:
            z_meta(source, 0, z).wait_recv()
            send_ways(source, lambda way, to: z_meta(source, way, to).start())
            c_meta(source, core).start()
        for part in range(PIECES):
            for source in arriving:
                z_copy(source, 0, z, part).wait_recv()
                send_ways(source, lambda way, to: z_copy(source, way, to, part).start())
                c_copy(source, core, part).start()

    orders = [arrival_order(place, planes) for place in range(planes)]

    def source_at(turn):
        source = jnp.int32(orders[0][turn])
        for place in range(1, planes):
            source = jnp.where(z == place, orders[place][turn], source)
        return source

    sources = [source_at(turn) for turn in range(planes - 1)]
    inner = has_low & has_high
    final = sources[-1]

    def at_end(source):
        @pl.when(jnp.logical_not(inner))
        def _():
            take(source)

    column_of(0)
    wait_partner(z)
    absorb(0, 1, z, True)

    @pl.when(inner)
    def _():
        take(*sources[:2])
        for source in sources[2:]:
            take(source)

    for source in sources[:-1]:
        at_end(source)
        wait_partner(source)
        absorb(0, 1, source, False)

    for spot in range(1, spots):
        q_meta(seen_from(spot)).wait_recv()
        column_of(spot)
        q_copy(seen_from(spot)).wait_recv()
    absorb(1, spots, z, True)
    for source in sources[:-1]:
        absorb(1, spots, source, False)
    at_end(final)
    wait_partner(final)

    def stat_rows(spot):
        top = jnp.max(jnp.transpose(peak[spot]), axis=0, keepdims=True)
        mass = jnp.sum(jnp.transpose(weight[spot]), axis=0, keepdims=True)
        return top, mass

    across, along = columns, 1
    corner = across + along
    half = rows // 2
    halves = (pl.ds(0, half), pl.ds(half, half))

    def p_copy(spot, side):
        mine = seen_from(spot)
        return remote(
            part_out.at[spot, halves[side]], part_in.at[mine, halves[side]],
            p_send.at[spot, side], p_recv.at[mine, side], spot_device(spot),
        )

    def corner_copy(side):
        spot = (along, across)[side]
        return remote(
            part_out.at[corner, halves[side]], part_in.at[corner, halves[side]],
            p_send.at[corner, side], p_recv.at[corner, side], spot_device(spot),
        )

    def s_copy(spot):
        mine = seen_from(spot)
        return remote(
            stat_out.at[spot], stat_in.at[mine], s_send.at[spot], s_recv.at[mine],
            spot_device(spot),
        )

    absorb(corner, corner + 1, final, False)
    part_out[corner] = total[corner].astype(jnp.bfloat16)
    corner_copy(0).start()
    corner_copy(1).start()
    passing = ((along, 1), (across, 0))
    for spot, side in passing:
        absorb(spot, spot + 1, final, False)
        part_out[spot, halves[1 - side]] = total[spot, halves[1 - side]].astype(jnp.bfloat16)
        p_copy(spot, 1 - side).start()
    for spot in range(spots - 1, 0, -1):
        stat_out[spot] = jnp.concatenate(stat_rows(spot), axis=0)
        s_copy(spot).start()
    for spot, side in passing:
        corner_copy(side).wait_recv()
        part_out[spot, halves[side]] = (
            total[spot, halves[side]] + part_in[corner, halves[side]].astype(jnp.float32)
        ).astype(jnp.bfloat16)
        p_copy(spot, side).start()

    absorb(0, 1, final, False)
    top, mass = stat_rows(0)
    total[0] += queries[0].astype(jnp.float32)
    for spot in range(1, spots):
        s_copy(seen_from(spot)).wait_recv()
        top = jnp.maximum(top, stat_in[spot, 0:1, :])
        mass = mass + stat_in[spot, 1:2, :]
    best_ref[...] = top.astype(jnp.bfloat16)
    below = jnp.transpose(jnp.broadcast_to(1.0 + mass, (rows, rows)))[:, 0:1]
    for spot, _ in passing:
        for side in range(2):
            p_copy(seen_from(spot), side).wait_recv()
    result = total[0]
    for spot, _ in passing:
        result = result + part_in[spot].astype(jnp.float32)
    mean_ref[...] = (result / below).astype(jnp.bfloat16)

    send_ways(z, lambda way, to: z_meta(z, way, to).wait_send())
    for part in range(PIECES):
        send_ways(z, lambda way, to: z_copy(z, way, to, part).wait_send())
    c_meta(z, core).wait_send()
    for part in range(PIECES):
        c_copy(z, core, part).wait_send()
    for source in sources:
        send_ways(source, lambda way, to: z_meta(source, way, to).wait_send())
        c_meta(source, core).wait_send()
        for part in range(PIECES):
            send_ways(source, lambda way, to: z_copy(source, way, to, part).wait_send())
            c_copy(source, core, part).wait_send()
    for spot in range(1, spots):
        q_meta(spot).wait_send()
        q_copy(spot).wait_send()
        s_copy(spot).wait_send()
    for side in range(2):
        corner_copy(side).wait_send()
        for spot, _ in passing:
            p_copy(spot, side).wait_send()


def dense(embeddings, bucket_ids, valid_rows):
    rows, features = embeddings.shape
    planes = lax.axis_size("wide") // PAIR
    spots = lax.axis_size("blk")
    dma = pltpu.SemaphoreType.DMA
    vmem = pl.BlockSpec(memory_space=pltpu.VMEM)
    mean, best = pl.pallas_call(
        functools.partial(dense_kernel, planes),
        out_shape=(
            jax.ShapeDtypeStruct((rows, features), jnp.bfloat16),
            jax.ShapeDtypeStruct((1, rows), jnp.bfloat16),
        ),
        in_specs=[vmem] * 3,
        out_specs=(vmem, vmem),
        scratch_shapes=[
            pltpu.VMEM((planes, PAIR, rows, features), jnp.bfloat16),
            pltpu.VMEM((planes, PAIR, 2, rows), jnp.float32),
            pltpu.VMEM((spots, rows, features), jnp.bfloat16),
            pltpu.VMEM((spots, 2, rows), jnp.float32),
            pltpu.VMEM((spots, rows, rows), jnp.float32),
            pltpu.VMEM((spots, rows, features), jnp.float32),
            pltpu.VMEM((spots, rows, rows), jnp.float32),
            pltpu.VMEM((spots, rows, rows), jnp.float32),
            pltpu.VMEM((spots, rows, features), jnp.bfloat16),
            pltpu.VMEM((spots, rows, features), jnp.bfloat16),
            pltpu.VMEM((spots, 2, rows), jnp.float32),
            pltpu.VMEM((spots, 2, rows), jnp.float32),
            dma((planes, 2, PIECES)), dma((planes, PIECES)), dma((planes, 2)), dma((planes,)),
            dma((planes, PIECES)), dma((planes, PIECES)), dma((planes,)), dma((planes,)),
            dma((spots,)), dma((spots,)), dma((spots,)), dma((spots,)),
            dma((spots, 2)), dma((spots, 2)), dma((spots,)), dma((spots,)),
        ],
        compiler_params=pltpu.CompilerParams(
            collective_id=0, has_side_effects=True, vmem_limit_bytes=16 * 1024 * 1024
        ),
    )(embeddings, bucket_ids.reshape(1, rows), valid_rows.reshape(1, rows))
    return mean, best.reshape(rows)


def on_device(embeddings, bucket_ids, slot_ids, valid_rows):
    rows = embeddings.shape[0]
    groups = lax.axis_size("wide")
    blocks = lax.axis_size("blk")
    bucket_work = blocks * (2 * rows) ** 2
    dense_work = groups * blocks * rows**2
    fits = groups % PAIR == 0 and groups > PAIR and blocks == PAIR * PAIR and rows == 128
    if fits and dense_work <= 4 * bucket_work:
        return dense(embeddings, bucket_ids, valid_rows)
    return by_bucket(embeddings, bucket_ids, slot_ids, valid_rows)


def solution(mesh):
    in_specs = (
        P(("wide", "blk"), None),
        P(("wide", "blk")),
        P(("wide", "blk")),
        P(("wide", "blk")),
    )
    out_specs = (P(("wide", "blk"), None), P(("wide", "blk")))
    return jax.shard_map(
        on_device, mesh=mesh, in_specs=in_specs, out_specs=out_specs, check_vma=False
    )
```

```python
import functools

import jax
import jax.numpy as jnp
from jax import lax
from jax.experimental import pallas as pl
from jax.experimental.pallas import tpu as pltpu
from jax.sharding import PartitionSpec as P

sharpness = 10.0


def from_behind(value, axis, steps):
    count = lax.axis_size(axis)
    pairs = [(source, (source + steps) % count) for source in range(count)]
    return lax.ppermute(value, axis, pairs)


def unit_rows(embeddings):
    float_rows = embeddings.astype(jnp.float32)
    inverse_norm = lax.rsqrt(jnp.mean(float_rows * float_rows, axis=1, keepdims=True) + 1e-06)
    return (float_rows * inverse_norm).astype(jnp.bfloat16)


def bucket_stats(queries, query_pos, key_rows, key_flags, key_pos):
    feature_count = queries.shape[1]
    cosine = (
        lax.dot_general(
            queries, key_rows, (((1,), (1,)), ((), ())), preferred_element_type=jnp.float32
        )
        / feature_count
    )
    usable = (key_flags[None, :] > 0) & (query_pos[:, None] != key_pos[None, :])
    best_cos = jnp.max(jnp.where(usable, cosine, -1.0), axis=1)
    weights = jnp.where(usable, jnp.exp(sharpness * (cosine - 1.0)), 0.0)
    weight_total = jnp.sum(weights, axis=1)
    summed = jnp.dot(weights.astype(jnp.bfloat16), key_rows, preferred_element_type=jnp.float32)
    return (best_cos, weight_total, summed)


def by_bucket(embeddings, bucket_ids, slot_ids, valid_rows):
    unit_vectors = unit_rows(embeddings)
    row_count, feature_count = unit_vectors.shape
    groups = lax.axis_size("wide")
    blocks = lax.axis_size("blk")
    slot_count = 2 * row_count // groups
    block_rows = groups * slot_count
    cell_ids = bucket_ids * slot_count + slot_ids
    outgoing = jnp.zeros((block_rows, feature_count), jnp.bfloat16).at[cell_ids].set(unit_vectors)
    flag_rows = (
        jnp.zeros((block_rows,), jnp.bfloat16).at[cell_ids].set(valid_rows.astype(jnp.bfloat16))
    )
    arrived, arrived_flags = (
        lax.all_to_all(
            outgoing.reshape(groups, slot_count, feature_count),
            "wide",
            split_axis=0,
            concat_axis=0,
            tiled=True,
        ),
        lax.all_to_all(
            flag_rows.reshape(groups, slot_count), "wide", split_axis=0, concat_axis=0, tiled=True
        ),
    )
    queries = arrived.reshape(block_rows, feature_count)
    query_flags = arrived_flags.reshape(block_rows)
    my_block = lax.axis_index("blk")
    query_pos = my_block * block_rows + jnp.arange(block_rows, dtype=jnp.int32)

    def absorb(running, key_rows, key_flags, key_start):
        key_pos = key_start + jnp.arange(key_rows.shape[0], dtype=jnp.int32)
        best_cos, weight_total, summed = bucket_stats(
            queries, query_pos, key_rows, key_flags, key_pos
        )
        return (jnp.maximum(running[0], best_cos), running[1] + weight_total, running[2] + summed)

    initial = (
        jnp.full((block_rows,), -1.0, jnp.float32),
        jnp.zeros((block_rows,), jnp.float32),
        jnp.zeros((block_rows, feature_count), jnp.float32),
    )
    key_rows, key_flags = (queries, query_flags)
    running = absorb(initial, key_rows, key_flags, my_block * block_rows)
    for turn_index in range(1, blocks):
        key_rows, key_flags = from_behind((key_rows, key_flags), "blk", 1)
        running = absorb(
            running, key_rows, key_flags, (my_block - turn_index) % blocks * block_rows
        )
    best_cos, weight_total, summed = running
    mean_rows = ((queries.astype(jnp.float32) + summed) / (1.0 + weight_total[:, None])).astype(
        jnp.bfloat16
    )
    back_mean, back_best = (
        lax.all_to_all(
            mean_rows.reshape(groups, slot_count, feature_count),
            "wide",
            split_axis=0,
            concat_axis=0,
            tiled=True,
        ),
        lax.all_to_all(
            best_cos.astype(jnp.bfloat16).reshape(groups, slot_count),
            "wide",
            split_axis=0,
            concat_axis=0,
            tiled=True,
        ),
    )
    neighbour_mean = back_mean.reshape(block_rows, feature_count)[cell_ids]
    max_cosine = back_best.reshape(block_rows)[cell_ids]
    return (neighbour_mean, max_cosine)


PAIR = 2
PIECES = 4


def arrival_order(place, count):
    low, high = place, count - 1 - place
    order = []
    for distance in range(1, count):
        if distance <= low:
            order.append(place - distance)
        if distance <= high:
            order.append(place + distance)
    return order


def dense_kernel(
    planes, emb_hbm, bucket_hbm, valid_hbm, mean_ref, best_ref,
    emb_ref, bucket_ref, valid_ref, load_sem,
    keys, key_meta, queries, query_meta, query_col, total, peak, weight,
    part_out, part_in, stat_out, stat_in,
    z_send, z_recv, zm_send, zm_recv, c_send, c_recv, cm_send, cm_recv,
    q_send, q_recv, qm_send, qm_recv, p_send, p_recv, s_send, s_recv,
):
    rows, features = emb_ref.shape
    spots = queries.shape[0]
    wide, blk = lax.axis_index("wide"), lax.axis_index("blk")
    z, y = lax.div(wide, PAIR), lax.rem(wide, PAIR)
    x, core = lax.div(blk, PAIR), lax.rem(blk, PAIR)
    other = 1 - core
    columns = spots // PAIR
    piece = rows // PIECES

    def at(z_at, y_at, x_at, core_at):
        return (z_at * PAIR + y_at, x_at * PAIR + core_at)

    def spot_device(spot):
        dy, dx = divmod(spot, columns)
        return at(z, lax.rem(y + dy, PAIR), lax.rem(x + dx, columns), core)

    def seen_from(spot):
        dy, dx = divmod(spot, columns)
        return (-dy) % PAIR * columns + (-dx) % columns

    def remote(source, target, send, recv, device):
        return pltpu.make_async_remote_copy(
            src_ref=source, dst_ref=target, send_sem=send, recv_sem=recv,
            device_id=device, device_id_type=pl.DeviceIdType.MESH,
        )

    partner = at(z, y, x, other)
    has_low, has_high = z > 0, z < planes - 1

    loads = [
        pltpu.make_async_copy(source, target, load_sem.at[index])
        for index, (source, target) in enumerate(
            ((emb_hbm, emb_ref), (bucket_hbm, bucket_ref), (valid_hbm, valid_ref))
        )
    ]
    for load in loads:
        load.start()

    barrier = pltpu.get_barrier_semaphore()

    def greet(device):
        pl.semaphore_signal(barrier, inc=1, device_id=device, device_id_type=pl.DeviceIdType.MESH)

    greet(partner)
    for spot in range(1, spots):
        greet(spot_device(spot))

    @pl.when(has_low)
    def _():
        greet(at(z - 1, y, x, core))

    @pl.when(has_high)
    def _():
        greet(at(z + 1, y, x, core))

    for load in loads:
        load.wait()
    floats = emb_ref[...].astype(jnp.float32)
    inverse = lax.rsqrt(jnp.mean(floats * floats, axis=1, keepdims=True) + 1e-06)
    unit = (floats * inverse).astype(jnp.bfloat16)
    keys[z, core] = unit
    queries[0] = unit
    meta = jnp.concatenate([bucket_ref[...], valid_ref[...]], axis=0).astype(jnp.float32)
    key_meta[z, core] = meta
    query_meta[0] = meta

    pl.semaphore_wait(barrier, jnp.where(has_low & has_high, spots + 2, spots + 1))

    def z_meta(source, way, to):
        ref = key_meta.at[source, core]
        return remote(
            ref, ref, zm_send.at[source, way], zm_recv.at[source], at(to, y, x, core)
        )

    def z_copy(source, way, to, part):
        ref = keys.at[source, core, pl.ds(part * piece, piece)]
        return remote(
            ref, ref, z_send.at[source, way, part], z_recv.at[source, part], at(to, y, x, core)
        )

    def c_meta(source, side):
        ref = key_meta.at[source, side]
        return remote(ref, ref, cm_send.at[source], cm_recv.at[source], partner)

    def c_copy(source, side, part):
        ref = keys.at[source, side, pl.ds(part * piece, piece)]
        return remote(ref, ref, c_send.at[source, part], c_recv.at[source, part], partner)

    def q_meta(spot):
        mine = seen_from(spot)
        return remote(
            query_meta.at[0], query_meta.at[mine], qm_send.at[spot], qm_recv.at[mine],
            spot_device(spot),
        )

    def q_copy(spot):
        mine = seen_from(spot)
        return remote(
            queries.at[0], queries.at[mine], q_send.at[spot], q_recv.at[mine], spot_device(spot)
        )

    def send_ways(source, act):
        @pl.when((source <= z) & has_high)
        def _():
            act(1, z + 1)

        @pl.when((source >= z) & has_low)
        def _():
            act(0, z - 1)

    send_ways(z, lambda way, to: z_meta(z, way, to).start())
    for part in range(PIECES):
        send_ways(z, lambda way, to: z_copy(z, way, to, part).start())
    c_meta(z, core).start()
    for part in range(PIECES):
        c_copy(z, core, part).start()
    for spot in range(spots - 1, 0, -1):
        q_meta(spot).start()
        q_copy(spot).start()

    def column_of(spot):
        row = query_meta[spot, 0:1, :]
        query_col[spot] = jnp.transpose(jnp.broadcast_to(row, (rows, rows)))

    def absorb(first, last, source, fresh):
        count = (last - first) * rows
        chosen = queries[first:last].reshape(count, features)
        block = keys[source].reshape(PAIR * rows, features)
        cosine = lax.dot_general(
            chosen, block, (((1,), (1,)), ((), ())), preferred_element_type=jnp.float32
        ) * (1.0 / features)
        buckets = query_col[first:last].reshape(count, rows)
        line = lax.broadcasted_iota(jnp.int32, (count, rows), 0)
        lane = lax.broadcasted_iota(jnp.int32, (count, rows), 1)
        factors = []
        peaks = None
        sums = None
        for side in range(PAIR):
            key_bucket = key_meta[source, side, 0:1, :]
            key_flag = key_meta[source, side, 1:2, :]
            wanted = jnp.where(key_flag > 0, key_bucket, -1.0)
            usable = buckets == wanted
            if first == 0:
                own = (source == z) & (core == side)
                shift = jnp.where(own, 0, count + rows)
                usable = usable & (line + shift != lane)
            values = cosine[:, side * rows : (side + 1) * rows]
            best = jnp.where(usable, values, -1.0)
            factor = jnp.where(usable, jnp.exp(sharpness * (values - 1.0)), 0.0)
            factors.append(factor.astype(jnp.bfloat16))
            peaks = best if peaks is None else jnp.maximum(peaks, best)
            sums = factor if sums is None else sums + factor
        summed = jnp.dot(
            jnp.concatenate(factors, axis=1), block, preferred_element_type=jnp.float32
        )
        part = (last - first, rows)
        if fresh:
            peak[first:last] = peaks.reshape(*part, rows)
            weight[first:last] = sums.reshape(*part, rows)
            total[first:last] = summed.reshape(*part, features)
        else:
            peak[first:last] = jnp.maximum(peak[first:last], peaks.reshape(*part, rows))
            weight[first:last] += sums.reshape(*part, rows)
            total[first:last] += summed.reshape(*part, features)

    def wait_partner(source):
        c_meta(source, other).wait_recv()
        for part in range(PIECES):
            c_copy(source, other, part).wait_recv()

    def take(*arriving):
        for source in arriving:
            z_meta(source, 0, z).wait_recv()
            send_ways(source, lambda way, to: z_meta(source, way, to).start())
            c_meta(source, core).start()
        for part in range(PIECES):
            for source in arriving:
                z_copy(source, 0, z, part).wait_recv()
                send_ways(source, lambda way, to: z_copy(source, way, to, part).start())
                c_copy(source, core, part).start()

    orders = [arrival_order(place, planes) for place in range(planes)]

    def source_at(turn):
        source = jnp.int32(orders[0][turn])
        for place in range(1, planes):
            source = jnp.where(z == place, orders[place][turn], source)
        return source

    sources = [source_at(turn) for turn in range(planes - 1)]
    inner = has_low & has_high
    final = sources[-1]

    def at_end(source):
        @pl.when(jnp.logical_not(inner))
        def _():
            take(source)

    column_of(0)
    wait_partner(z)
    absorb(0, 1, z, True)

    @pl.when(inner)
    def _():
        take(*sources[:2])
        for source in sources[2:]:
            take(source)

    for source in sources[:-1]:
        at_end(source)
        wait_partner(source)
        absorb(0, 1, source, False)

    for spot in range(1, spots):
        q_meta(seen_from(spot)).wait_recv()
        column_of(spot)
        q_copy(seen_from(spot)).wait_recv()
    absorb(1, spots, z, True)
    for source in sources[:-1]:
        absorb(1, spots, source, False)
    at_end(final)
    wait_partner(final)

    def stat_rows(spot):
        top = jnp.max(jnp.transpose(peak[spot]), axis=0, keepdims=True)
        mass = jnp.sum(jnp.transpose(weight[spot]), axis=0, keepdims=True)
        return top, mass

    across, along = columns, 1
    corner = across + along
    half = rows // 2
    halves = (pl.ds(0, half), pl.ds(half, half))

    def p_copy(spot, side):
        mine = seen_from(spot)
        return remote(
            part_out.at[spot, halves[side]], part_in.at[mine, halves[side]],
            p_send.at[spot, side], p_recv.at[mine, side], spot_device(spot),
        )

    def corner_copy(side):
        spot = (along, across)[side]
        return remote(
            part_out.at[corner, halves[side]], part_in.at[corner, halves[side]],
            p_send.at[corner, side], p_recv.at[corner, side], spot_device(spot),
        )

    def s_copy(spot):
        mine = seen_from(spot)
        return remote(
            stat_out.at[spot], stat_in.at[mine], s_send.at[spot], s_recv.at[mine],
            spot_device(spot),
        )

    absorb(corner, corner + 1, final, False)
    part_out[corner] = total[corner].astype(jnp.bfloat16)
    corner_copy(0).start()
    corner_copy(1).start()
    passing = ((along, 1), (across, 0))
    for spot, side in passing:
        absorb(spot, spot + 1, final, False)
        part_out[spot, halves[1 - side]] = total[spot, halves[1 - side]].astype(jnp.bfloat16)
        p_copy(spot, 1 - side).start()
    for spot in range(spots - 1, 0, -1):
        stat_out[spot] = jnp.concatenate(stat_rows(spot), axis=0)
        s_copy(spot).start()
    for spot, side in passing:
        corner_copy(side).wait_recv()
        part_out[spot, halves[side]] = (
            total[spot, halves[side]] + part_in[corner, halves[side]].astype(jnp.float32)
        ).astype(jnp.bfloat16)
        p_copy(spot, side).start()

    absorb(0, 1, final, False)
    top, mass = stat_rows(0)
    total[0] += queries[0].astype(jnp.float32)
    for spot in range(1, spots):
        s_copy(seen_from(spot)).wait_recv()
        top = jnp.maximum(top, stat_in[spot, 0:1, :])
        mass = mass + stat_in[spot, 1:2, :]
    best_ref[...] = top.astype(jnp.bfloat16)
    below = jnp.transpose(jnp.broadcast_to(1.0 + mass, (rows, rows)))[:, 0:1]
    for spot, _ in passing:
        for side in range(2):
            p_copy(seen_from(spot), side).wait_recv()
    result = total[0]
    for spot, _ in passing:
        result = result + part_in[spot].astype(jnp.float32)
    mean_ref[...] = (result / below).astype(jnp.bfloat16)

    send_ways(z, lambda way, to: z_meta(z, way, to).wait_send())
    for part in range(PIECES):
        send_ways(z, lambda way, to: z_copy(z, way, to, part).wait_send())
    c_meta(z, core).wait_send()
    for part in range(PIECES):
        c_copy(z, core, part).wait_send()
    for source in sources:
        send_ways(source, lambda way, to: z_meta(source, way, to).wait_send())
        c_meta(source, core).wait_send()
        for part in range(PIECES):
            send_ways(source, lambda way, to: z_copy(source, way, to, part).wait_send())
            c_copy(source, core, part).wait_send()
    for spot in range(1, spots):
        q_meta(spot).wait_send()
        q_copy(spot).wait_send()
        s_copy(spot).wait_send()
    for side in range(2):
        corner_copy(side).wait_send()
        for spot, _ in passing:
            p_copy(spot, side).wait_send()


def dense(embeddings, bucket_ids, valid_rows):
    rows, features = embeddings.shape
    planes = lax.axis_size("wide") // PAIR
    spots = lax.axis_size("blk")
    dma = pltpu.SemaphoreType.DMA
    vmem = pl.BlockSpec(memory_space=pltpu.VMEM)
    mean, best = pl.pallas_call(
        functools.partial(dense_kernel, planes),
        out_shape=(
            jax.ShapeDtypeStruct((rows, features), jnp.bfloat16),
            jax.ShapeDtypeStruct((1, rows), jnp.bfloat16),
        ),
        in_specs=[pl.BlockSpec(memory_space=pltpu.HBM)] * 3,
        out_specs=(vmem, vmem),
        scratch_shapes=[
            pltpu.VMEM((rows, features), jnp.bfloat16),
            pltpu.VMEM((1, rows), jnp.int32),
            pltpu.VMEM((1, rows), jnp.int32),
            dma((3,)),
            pltpu.VMEM((planes, PAIR, rows, features), jnp.bfloat16),
            pltpu.VMEM((planes, PAIR, 2, rows), jnp.float32),
            pltpu.VMEM((spots, rows, features), jnp.bfloat16),
            pltpu.VMEM((spots, 2, rows), jnp.float32),
            pltpu.VMEM((spots, rows, rows), jnp.float32),
            pltpu.VMEM((spots, rows, features), jnp.float32),
            pltpu.VMEM((spots, rows, rows), jnp.float32),
            pltpu.VMEM((spots, rows, rows), jnp.float32),
            pltpu.VMEM((spots, rows, features), jnp.bfloat16),
            pltpu.VMEM((spots, rows, features), jnp.bfloat16),
            pltpu.VMEM((spots, 2, rows), jnp.float32),
            pltpu.VMEM((spots, 2, rows), jnp.float32),
            dma((planes, 2, PIECES)), dma((planes, PIECES)), dma((planes, 2)), dma((planes,)),
            dma((planes, PIECES)), dma((planes, PIECES)), dma((planes,)), dma((planes,)),
            dma((spots,)), dma((spots,)), dma((spots,)), dma((spots,)),
            dma((spots, 2)), dma((spots, 2)), dma((spots,)), dma((spots,)),
        ],
        compiler_params=pltpu.CompilerParams(
            collective_id=0, has_side_effects=True, vmem_limit_bytes=16 * 1024 * 1024
        ),
    )(embeddings, bucket_ids.reshape(1, rows), valid_rows.reshape(1, rows))
    return mean, best.reshape(rows)


def on_device(embeddings, bucket_ids, slot_ids, valid_rows):
    rows = embeddings.shape[0]
    groups = lax.axis_size("wide")
    blocks = lax.axis_size("blk")
    bucket_work = blocks * (2 * rows) ** 2
    dense_work = groups * blocks * rows**2
    fits = groups % PAIR == 0 and groups > PAIR and blocks == PAIR * PAIR and rows == 128
    if fits and dense_work <= 4 * bucket_work:
        return dense(embeddings, bucket_ids, valid_rows)
    return by_bucket(embeddings, bucket_ids, slot_ids, valid_rows)


def solution(mesh):
    in_specs = (
        P(("wide", "blk"), None),
        P(("wide", "blk")),
        P(("wide", "blk")),
        P(("wide", "blk")),
    )
    out_specs = (P(("wide", "blk"), None), P(("wide", "blk")))
    return jax.shard_map(
        on_device, mesh=mesh, in_specs=in_specs, out_specs=out_specs, check_vma=False
    )
```

```python
import functools

import jax
import jax.numpy as jnp
from jax import lax
from jax.experimental import pallas as pl
from jax.experimental.pallas import tpu as pltpu
from jax.sharding import PartitionSpec as P

sharpness = 10.0


def from_behind(value, axis, steps):
    count = lax.axis_size(axis)
    pairs = [(source, (source + steps) % count) for source in range(count)]
    return lax.ppermute(value, axis, pairs)


def unit_rows(embeddings):
    float_rows = embeddings.astype(jnp.float32)
    inverse_norm = lax.rsqrt(jnp.mean(float_rows * float_rows, axis=1, keepdims=True) + 1e-06)
    return (float_rows * inverse_norm).astype(jnp.bfloat16)


def bucket_stats(queries, query_pos, key_rows, key_flags, key_pos):
    feature_count = queries.shape[1]
    cosine = (
        lax.dot_general(
            queries, key_rows, (((1,), (1,)), ((), ())), preferred_element_type=jnp.float32
        )
        / feature_count
    )
    usable = (key_flags[None, :] > 0) & (query_pos[:, None] != key_pos[None, :])
    best_cos = jnp.max(jnp.where(usable, cosine, -1.0), axis=1)
    weights = jnp.where(usable, jnp.exp(sharpness * (cosine - 1.0)), 0.0)
    weight_total = jnp.sum(weights, axis=1)
    summed = jnp.dot(weights.astype(jnp.bfloat16), key_rows, preferred_element_type=jnp.float32)
    return (best_cos, weight_total, summed)


def by_bucket(embeddings, bucket_ids, slot_ids, valid_rows):
    unit_vectors = unit_rows(embeddings)
    row_count, feature_count = unit_vectors.shape
    groups = lax.axis_size("wide")
    blocks = lax.axis_size("blk")
    slot_count = 2 * row_count // groups
    block_rows = groups * slot_count
    cell_ids = bucket_ids * slot_count + slot_ids
    outgoing = jnp.zeros((block_rows, feature_count), jnp.bfloat16).at[cell_ids].set(unit_vectors)
    flag_rows = (
        jnp.zeros((block_rows,), jnp.bfloat16).at[cell_ids].set(valid_rows.astype(jnp.bfloat16))
    )
    arrived, arrived_flags = (
        lax.all_to_all(
            outgoing.reshape(groups, slot_count, feature_count),
            "wide",
            split_axis=0,
            concat_axis=0,
            tiled=True,
        ),
        lax.all_to_all(
            flag_rows.reshape(groups, slot_count), "wide", split_axis=0, concat_axis=0, tiled=True
        ),
    )
    queries = arrived.reshape(block_rows, feature_count)
    query_flags = arrived_flags.reshape(block_rows)
    my_block = lax.axis_index("blk")
    query_pos = my_block * block_rows + jnp.arange(block_rows, dtype=jnp.int32)

    def absorb(running, key_rows, key_flags, key_start):
        key_pos = key_start + jnp.arange(key_rows.shape[0], dtype=jnp.int32)
        best_cos, weight_total, summed = bucket_stats(
            queries, query_pos, key_rows, key_flags, key_pos
        )
        return (jnp.maximum(running[0], best_cos), running[1] + weight_total, running[2] + summed)

    initial = (
        jnp.full((block_rows,), -1.0, jnp.float32),
        jnp.zeros((block_rows,), jnp.float32),
        jnp.zeros((block_rows, feature_count), jnp.float32),
    )
    key_rows, key_flags = (queries, query_flags)
    running = absorb(initial, key_rows, key_flags, my_block * block_rows)
    for turn_index in range(1, blocks):
        key_rows, key_flags = from_behind((key_rows, key_flags), "blk", 1)
        running = absorb(
            running, key_rows, key_flags, (my_block - turn_index) % blocks * block_rows
        )
    best_cos, weight_total, summed = running
    mean_rows = ((queries.astype(jnp.float32) + summed) / (1.0 + weight_total[:, None])).astype(
        jnp.bfloat16
    )
    back_mean, back_best = (
        lax.all_to_all(
            mean_rows.reshape(groups, slot_count, feature_count),
            "wide",
            split_axis=0,
            concat_axis=0,
            tiled=True,
        ),
        lax.all_to_all(
            best_cos.astype(jnp.bfloat16).reshape(groups, slot_count),
            "wide",
            split_axis=0,
            concat_axis=0,
            tiled=True,
        ),
    )
    neighbour_mean = back_mean.reshape(block_rows, feature_count)[cell_ids]
    max_cosine = back_best.reshape(block_rows)[cell_ids]
    return (neighbour_mean, max_cosine)


PAIR = 2
PIECES = 4
GRANT = 56_240_000


def arrival_order(place, count):
    low, high = place, count - 1 - place
    order = []
    for distance in range(1, count):
        if distance <= low:
            order.append(place - distance)
        if distance <= high:
            order.append(place + distance)
    return order


def dense_kernel(
    planes, emb_hbm, bucket_hbm, valid_hbm, mean_ref, best_ref,
    emb_ref, bucket_ref, valid_ref, load_sem,
    keys, key_meta, queries, query_meta, query_col, total, peak, weight,
    part_out, part_in, stat_out, stat_in,
    z_send, z_recv, zm_send, zm_recv, c_send, c_recv, cm_send, cm_recv,
    q_send, q_recv, qm_send, qm_recv, p_send, p_recv, s_send, s_recv,
):
    rows, features = emb_ref.shape
    spots = queries.shape[0]
    wide, blk = lax.axis_index("wide"), lax.axis_index("blk")
    z, y = lax.div(wide, PAIR), lax.rem(wide, PAIR)
    x, core = lax.div(blk, PAIR), lax.rem(blk, PAIR)
    other = 1 - core
    columns = spots // PAIR
    piece = rows // PIECES

    def at(z_at, y_at, x_at, core_at):
        return (z_at * PAIR + y_at, x_at * PAIR + core_at)

    def spot_device(spot):
        dy, dx = divmod(spot, columns)
        return at(z, lax.rem(y + dy, PAIR), lax.rem(x + dx, columns), core)

    def seen_from(spot):
        dy, dx = divmod(spot, columns)
        return (-dy) % PAIR * columns + (-dx) % columns

    def remote(source, target, send, recv, device):
        return pltpu.make_async_remote_copy(
            src_ref=source, dst_ref=target, send_sem=send, recv_sem=recv,
            device_id=device, device_id_type=pl.DeviceIdType.MESH,
        )

    partner = at(z, y, x, other)
    has_low, has_high = z > 0, z < planes - 1

    loads = [
        pltpu.make_async_copy(source, target, load_sem.at[index])
        for index, (source, target) in enumerate(
            ((emb_hbm, emb_ref), (bucket_hbm, bucket_ref), (valid_hbm, valid_ref))
        )
    ]
    for load in loads:
        load.start()

    barrier = pltpu.get_barrier_semaphore()

    def greet(device):
        pl.semaphore_signal(barrier, inc=1, device_id=device, device_id_type=pl.DeviceIdType.MESH)

    greet(partner)
    for spot in range(1, spots):
        greet(spot_device(spot))

    @pl.when(has_low)
    def _():
        greet(at(z - 1, y, x, core))

    @pl.when(has_high)
    def _():
        greet(at(z + 1, y, x, core))

    for load in loads:
        load.wait()
    floats = emb_ref[...].astype(jnp.float32)
    inverse = lax.rsqrt(jnp.mean(floats * floats, axis=1, keepdims=True) + 1e-06)
    unit = (floats * inverse).astype(jnp.bfloat16)
    keys[z, core] = unit
    queries[0] = unit
    meta = jnp.concatenate([bucket_ref[...], valid_ref[...]], axis=0).astype(jnp.float32)
    key_meta[z, core] = meta
    query_meta[0] = meta

    pl.semaphore_wait(barrier, jnp.where(has_low & has_high, spots + 2, spots + 1))

    def z_meta(source, way, to):
        ref = key_meta.at[source, core]
        return remote(
            ref, ref, zm_send.at[source, way], zm_recv.at[source], at(to, y, x, core)
        )

    def z_copy(source, way, to, part):
        ref = keys.at[source, core, pl.ds(part * piece, piece)]
        return remote(
            ref, ref, z_send.at[source, way, part], z_recv.at[source, part], at(to, y, x, core)
        )

    def c_meta(source, side):
        ref = key_meta.at[source, side]
        return remote(ref, ref, cm_send.at[source], cm_recv.at[source], partner)

    def c_copy(source, side, part):
        ref = keys.at[source, side, pl.ds(part * piece, piece)]
        return remote(ref, ref, c_send.at[source, part], c_recv.at[source, part], partner)

    def q_meta(spot):
        mine = seen_from(spot)
        return remote(
            query_meta.at[0], query_meta.at[mine], qm_send.at[spot], qm_recv.at[mine],
            spot_device(spot),
        )

    def q_copy(spot):
        mine = seen_from(spot)
        return remote(
            queries.at[0], queries.at[mine], q_send.at[spot], q_recv.at[mine], spot_device(spot)
        )

    def send_ways(source, act):
        @pl.when((source <= z) & has_high)
        def _():
            act(1, z + 1)

        @pl.when((source >= z) & has_low)
        def _():
            act(0, z - 1)

    send_ways(z, lambda way, to: z_meta(z, way, to).start())
    for part in range(PIECES):
        send_ways(z, lambda way, to: z_copy(z, way, to, part).start())
    c_meta(z, core).start()
    for part in range(PIECES):
        c_copy(z, core, part).start()
    for spot in range(spots - 1, 0, -1):
        q_meta(spot).start()
        q_copy(spot).start()

    def column_of(spot):
        row = query_meta[spot, 0:1, :]
        query_col[spot] = jnp.transpose(jnp.broadcast_to(row, (rows, rows)))

    def absorb(first, last, source, fresh, sides=tuple(range(PAIR))):
        count = (last - first) * rows
        chosen = queries[first:last].reshape(count, features)
        if len(sides) == PAIR:
            block = keys[source].reshape(PAIR * rows, features)
        else:
            block = keys[source, sides[0]]
        cosine = lax.dot_general(
            chosen, block, (((1,), (1,)), ((), ())), preferred_element_type=jnp.float32
        ) * (1.0 / features)
        buckets = query_col[first:last].reshape(count, rows)
        line = lax.broadcasted_iota(jnp.int32, (count, rows), 0)
        lane = lax.broadcasted_iota(jnp.int32, (count, rows), 1)
        factors = []
        peaks = None
        sums = None
        for index, side in enumerate(sides):
            key_bucket = key_meta[source, side, 0:1, :]
            key_flag = key_meta[source, side, 1:2, :]
            wanted = jnp.where(key_flag > 0, key_bucket, -1.0)
            usable = buckets == wanted
            if first == 0:
                own = (source == z) & (core == side)
                shift = jnp.where(own, 0, count + rows)
                usable = usable & (line + shift != lane)
            values = cosine[:, index * rows : (index + 1) * rows]
            best = jnp.where(usable, values, -1.0)
            factor = jnp.where(usable, jnp.exp(sharpness * (values - 1.0)), 0.0)
            factors.append(factor.astype(jnp.bfloat16))
            peaks = best if peaks is None else jnp.maximum(peaks, best)
            sums = factor if sums is None else sums + factor
        summed = jnp.dot(
            jnp.concatenate(factors, axis=1), block, preferred_element_type=jnp.float32
        )
        part = (last - first, rows)
        if fresh:
            peak[first:last] = peaks.reshape(*part, rows)
            weight[first:last] = sums.reshape(*part, rows)
            total[first:last] = summed.reshape(*part, features)
        else:
            peak[first:last] = jnp.maximum(peak[first:last], peaks.reshape(*part, rows))
            weight[first:last] += sums.reshape(*part, rows)
            total[first:last] += summed.reshape(*part, features)

    def wait_partner(source):
        c_meta(source, other).wait_recv()
        for part in range(PIECES):
            c_copy(source, other, part).wait_recv()

    def take(*arriving):
        for source in arriving:
            z_meta(source, 0, z).wait_recv()
            send_ways(source, lambda way, to: z_meta(source, way, to).start())
            c_meta(source, core).start()
        for part in range(PIECES):
            for source in arriving:
                z_copy(source, 0, z, part).wait_recv()
                send_ways(source, lambda way, to: z_copy(source, way, to, part).start())
                c_copy(source, core, part).start()

    orders = [arrival_order(place, planes) for place in range(planes)]

    def source_at(turn):
        source = jnp.int32(orders[0][turn])
        for place in range(1, planes):
            source = jnp.where(z == place, orders[place][turn], source)
        return source

    sources = [source_at(turn) for turn in range(planes - 1)]
    inner = has_low & has_high
    final = sources[-1]

    def at_end(source):
        @pl.when(jnp.logical_not(inner))
        def _():
            take(source)

    column_of(0)
    wait_partner(z)
    absorb(0, 1, z, True)

    @pl.when(inner)
    def _():
        take(*sources[:2])
        for source in sources[2:]:
            take(source)

    for source in sources[:-1]:
        at_end(source)
        wait_partner(source)
        absorb(0, 1, source, False)

    for spot in range(1, spots):
        q_meta(seen_from(spot)).wait_recv()
        column_of(spot)
        q_copy(seen_from(spot)).wait_recv()
    absorb(1, spots, z, True)
    for source in sources[:-1]:
        absorb(1, spots, source, False)
    at_end(final)
    absorb(1, spots, final, False, (core,))
    wait_partner(final)

    def stat_rows(spot):
        top = jnp.max(jnp.transpose(peak[spot]), axis=0, keepdims=True)
        mass = jnp.sum(jnp.transpose(weight[spot]), axis=0, keepdims=True)
        return top, mass

    across, along = columns, 1
    corner = across + along
    half = rows // 2
    halves = (pl.ds(0, half), pl.ds(half, half))

    def p_copy(spot, side):
        mine = seen_from(spot)
        return remote(
            part_out.at[spot, halves[side]], part_in.at[mine, halves[side]],
            p_send.at[spot, side], p_recv.at[mine, side], spot_device(spot),
        )

    def corner_copy(side):
        spot = (along, across)[side]
        return remote(
            part_out.at[corner, halves[side]], part_in.at[corner, halves[side]],
            p_send.at[corner, side], p_recv.at[corner, side], spot_device(spot),
        )

    def s_copy(spot):
        mine = seen_from(spot)
        return remote(
            stat_out.at[spot], stat_in.at[mine], s_send.at[spot], s_recv.at[mine],
            spot_device(spot),
        )

    absorb(corner, corner + 1, final, False, (other,))
    part_out[corner] = total[corner].astype(jnp.bfloat16)
    corner_copy(0).start()
    corner_copy(1).start()
    passing = ((along, 1), (across, 0))
    for spot, side in passing:
        absorb(spot, spot + 1, final, False, (other,))
        part_out[spot, halves[1 - side]] = total[spot, halves[1 - side]].astype(jnp.bfloat16)
        p_copy(spot, 1 - side).start()
    for spot in range(spots - 1, 0, -1):
        stat_out[spot] = jnp.concatenate(stat_rows(spot), axis=0)
        s_copy(spot).start()
    absorb(0, 1, final, False)
    top, mass = stat_rows(0)
    total[0] += queries[0].astype(jnp.float32)
    for spot, side in passing:
        corner_copy(side).wait_recv()
        part_out[spot, halves[side]] = (
            total[spot, halves[side]] + part_in[corner, halves[side]].astype(jnp.float32)
        ).astype(jnp.bfloat16)
        p_copy(spot, side).start()

    for spot in range(1, spots):
        s_copy(seen_from(spot)).wait_recv()
        top = jnp.maximum(top, stat_in[spot, 0:1, :])
        mass = mass + stat_in[spot, 1:2, :]
    best_ref[...] = top.astype(jnp.bfloat16)
    below = jnp.transpose(jnp.broadcast_to(1.0 + mass, (rows, rows)))[:, 0:1]
    for spot, _ in passing:
        for side in range(2):
            p_copy(seen_from(spot), side).wait_recv()
    result = total[0]
    for spot, _ in passing:
        result = result + part_in[spot].astype(jnp.float32)
    mean_ref[...] = (result / below).astype(jnp.bfloat16)

    send_ways(z, lambda way, to: z_meta(z, way, to).wait_send())
    for part in range(PIECES):
        send_ways(z, lambda way, to: z_copy(z, way, to, part).wait_send())
    c_meta(z, core).wait_send()
    for part in range(PIECES):
        c_copy(z, core, part).wait_send()
    for source in sources:
        send_ways(source, lambda way, to: z_meta(source, way, to).wait_send())
        c_meta(source, core).wait_send()
        for part in range(PIECES):
            send_ways(source, lambda way, to: z_copy(source, way, to, part).wait_send())
            c_copy(source, core, part).wait_send()
    for spot in range(1, spots):
        q_meta(spot).wait_send()
        q_copy(spot).wait_send()
        s_copy(spot).wait_send()
    for side in range(2):
        corner_copy(side).wait_send()
        for spot, _ in passing:
            p_copy(spot, side).wait_send()


def dense(embeddings, bucket_ids, valid_rows):
    rows, features = embeddings.shape
    planes = lax.axis_size("wide") // PAIR
    spots = lax.axis_size("blk")
    dma = pltpu.SemaphoreType.DMA
    vmem = pl.BlockSpec(memory_space=pltpu.VMEM)
    mean, best = pl.pallas_call(
        functools.partial(dense_kernel, planes),
        out_shape=(
            jax.ShapeDtypeStruct((rows, features), jnp.bfloat16),
            jax.ShapeDtypeStruct((1, rows), jnp.bfloat16),
        ),
        in_specs=[pl.BlockSpec(memory_space=pltpu.HBM)] * 3,
        out_specs=(vmem, vmem),
        scratch_shapes=[
            pltpu.VMEM((rows, features), jnp.bfloat16),
            pltpu.VMEM((1, rows), jnp.int32),
            pltpu.VMEM((1, rows), jnp.int32),
            dma((3,)),
            pltpu.VMEM((planes, PAIR, rows, features), jnp.bfloat16),
            pltpu.VMEM((planes, PAIR, 2, rows), jnp.float32),
            pltpu.VMEM((spots, rows, features), jnp.bfloat16),
            pltpu.VMEM((spots, 2, rows), jnp.float32),
            pltpu.VMEM((spots, rows, rows), jnp.float32),
            pltpu.VMEM((spots, rows, features), jnp.float32),
            pltpu.VMEM((spots, rows, rows), jnp.float32),
            pltpu.VMEM((spots, rows, rows), jnp.float32),
            pltpu.VMEM((spots, rows, features), jnp.bfloat16),
            pltpu.VMEM((spots, rows, features), jnp.bfloat16),
            pltpu.VMEM((spots, 2, rows), jnp.float32),
            pltpu.VMEM((spots, 2, rows), jnp.float32),
            dma((planes, 2, PIECES)), dma((planes, PIECES)), dma((planes, 2)), dma((planes,)),
            dma((planes, PIECES)), dma((planes, PIECES)), dma((planes,)), dma((planes,)),
            dma((spots,)), dma((spots,)), dma((spots,)), dma((spots,)),
            dma((spots, 2)), dma((spots, 2)), dma((spots,)), dma((spots,)),
        ],
        compiler_params=pltpu.CompilerParams(
            collective_id=0, has_side_effects=True, vmem_limit_bytes=GRANT
        ),
    )(embeddings, bucket_ids.reshape(1, rows), valid_rows.reshape(1, rows))
    return mean, best.reshape(rows)


def on_device(embeddings, bucket_ids, slot_ids, valid_rows):
    rows = embeddings.shape[0]
    groups = lax.axis_size("wide")
    blocks = lax.axis_size("blk")
    bucket_work = blocks * (2 * rows) ** 2
    dense_work = groups * blocks * rows**2
    fits = groups % PAIR == 0 and groups > PAIR and blocks == PAIR * PAIR and rows == 128
    if fits and dense_work <= 4 * bucket_work:
        return dense(embeddings, bucket_ids, valid_rows)
    return by_bucket(embeddings, bucket_ids, slot_ids, valid_rows)


def solution(mesh):
    in_specs = (
        P(("wide", "blk"), None),
        P(("wide", "blk")),
        P(("wide", "blk")),
        P(("wide", "blk")),
    )
    out_specs = (P(("wide", "blk"), None), P(("wide", "blk")))
    return jax.shard_map(
        on_device, mesh=mesh, in_specs=in_specs, out_specs=out_specs, check_vma=False
    )
```

```python
import functools

import jax
import jax.numpy as jnp
from jax import lax
from jax.experimental import pallas as pl
from jax.experimental.pallas import tpu as pltpu
from jax.sharding import PartitionSpec as P

sharpness = 10.0


def from_behind(value, axis, steps):
    count = lax.axis_size(axis)
    pairs = [(source, (source + steps) % count) for source in range(count)]
    return lax.ppermute(value, axis, pairs)


def unit_rows(embeddings):
    float_rows = embeddings.astype(jnp.float32)
    inverse_norm = lax.rsqrt(jnp.mean(float_rows * float_rows, axis=1, keepdims=True) + 1e-06)
    return (float_rows * inverse_norm).astype(jnp.bfloat16)


def bucket_stats(queries, query_pos, key_rows, key_flags, key_pos):
    feature_count = queries.shape[1]
    cosine = (
        lax.dot_general(
            queries, key_rows, (((1,), (1,)), ((), ())), preferred_element_type=jnp.float32
        )
        / feature_count
    )
    usable = (key_flags[None, :] > 0) & (query_pos[:, None] != key_pos[None, :])
    best_cos = jnp.max(jnp.where(usable, cosine, -1.0), axis=1)
    weights = jnp.where(usable, jnp.exp(sharpness * (cosine - 1.0)), 0.0)
    weight_total = jnp.sum(weights, axis=1)
    summed = jnp.dot(weights.astype(jnp.bfloat16), key_rows, preferred_element_type=jnp.float32)
    return (best_cos, weight_total, summed)


def by_bucket(embeddings, bucket_ids, slot_ids, valid_rows):
    unit_vectors = unit_rows(embeddings)
    row_count, feature_count = unit_vectors.shape
    groups = lax.axis_size("wide")
    blocks = lax.axis_size("blk")
    slot_count = 2 * row_count // groups
    block_rows = groups * slot_count
    cell_ids = bucket_ids * slot_count + slot_ids
    outgoing = jnp.zeros((block_rows, feature_count), jnp.bfloat16).at[cell_ids].set(unit_vectors)
    flag_rows = (
        jnp.zeros((block_rows,), jnp.bfloat16).at[cell_ids].set(valid_rows.astype(jnp.bfloat16))
    )
    arrived, arrived_flags = (
        lax.all_to_all(
            outgoing.reshape(groups, slot_count, feature_count),
            "wide",
            split_axis=0,
            concat_axis=0,
            tiled=True,
        ),
        lax.all_to_all(
            flag_rows.reshape(groups, slot_count), "wide", split_axis=0, concat_axis=0, tiled=True
        ),
    )
    queries = arrived.reshape(block_rows, feature_count)
    query_flags = arrived_flags.reshape(block_rows)
    my_block = lax.axis_index("blk")
    query_pos = my_block * block_rows + jnp.arange(block_rows, dtype=jnp.int32)

    def absorb(running, key_rows, key_flags, key_start):
        key_pos = key_start + jnp.arange(key_rows.shape[0], dtype=jnp.int32)
        best_cos, weight_total, summed = bucket_stats(
            queries, query_pos, key_rows, key_flags, key_pos
        )
        return (jnp.maximum(running[0], best_cos), running[1] + weight_total, running[2] + summed)

    initial = (
        jnp.full((block_rows,), -1.0, jnp.float32),
        jnp.zeros((block_rows,), jnp.float32),
        jnp.zeros((block_rows, feature_count), jnp.float32),
    )
    key_rows, key_flags = (queries, query_flags)
    running = absorb(initial, key_rows, key_flags, my_block * block_rows)
    for turn_index in range(1, blocks):
        key_rows, key_flags = from_behind((key_rows, key_flags), "blk", 1)
        running = absorb(
            running, key_rows, key_flags, (my_block - turn_index) % blocks * block_rows
        )
    best_cos, weight_total, summed = running
    mean_rows = ((queries.astype(jnp.float32) + summed) / (1.0 + weight_total[:, None])).astype(
        jnp.bfloat16
    )
    back_mean, back_best = (
        lax.all_to_all(
            mean_rows.reshape(groups, slot_count, feature_count),
            "wide",
            split_axis=0,
            concat_axis=0,
            tiled=True,
        ),
        lax.all_to_all(
            best_cos.astype(jnp.bfloat16).reshape(groups, slot_count),
            "wide",
            split_axis=0,
            concat_axis=0,
            tiled=True,
        ),
    )
    neighbour_mean = back_mean.reshape(block_rows, feature_count)[cell_ids]
    max_cosine = back_best.reshape(block_rows)[cell_ids]
    return (neighbour_mean, max_cosine)


PAIR = 2
PIECES = 4
GRANT = 56_240_000


def arrival_order(place, count):
    low, high = place, count - 1 - place
    order = []
    for distance in range(1, count):
        if distance <= low:
            order.append(place - distance)
        if distance <= high:
            order.append(place + distance)
    if low == 0 or high == 0:
        order = [order[1], order[1]] + order[2:]
    return order


def dense_kernel(
    planes, emb_hbm, bucket_hbm, valid_hbm, mean_ref, best_ref,
    emb_ref, bucket_ref, valid_ref, load_sem,
    keys, key_meta, queries, query_meta, query_col, total, peak, weight,
    part_out, part_in, stat_out, stat_in,
    plane_keys, plane_meta, help_total, help_peak, help_weight,
    help_out, help_in, help_stat_out, help_stat_in,
    z_send, z_recv, zm_send, zm_recv, c_send, c_recv, cm_send, cm_recv,
    q_send, q_recv, qm_send, qm_recv, p_send, p_recv, s_send, s_recv,
    f_send, f_recv, fm_send, fm_recv, h_send, h_recv,
):
    rows, features = emb_ref.shape
    spots = queries.shape[0]
    wide, blk = lax.axis_index("wide"), lax.axis_index("blk")
    z, y = lax.div(wide, PAIR), lax.rem(wide, PAIR)
    x, core = lax.div(blk, PAIR), lax.rem(blk, PAIR)
    other = 1 - core
    columns = spots // PAIR
    piece = rows // PIECES

    def at(z_at, y_at, x_at, core_at):
        return (z_at * PAIR + y_at, x_at * PAIR + core_at)

    def spot_device(spot):
        dy, dx = divmod(spot, columns)
        return at(z, lax.rem(y + dy, PAIR), lax.rem(x + dx, columns), core)

    def seen_from(spot):
        dy, dx = divmod(spot, columns)
        return (-dy) % PAIR * columns + (-dx) % columns

    def remote(source, target, send, recv, device):
        return pltpu.make_async_remote_copy(
            src_ref=source, dst_ref=target, send_sem=send, recv_sem=recv,
            device_id=device, device_id_type=pl.DeviceIdType.MESH,
        )

    partner = at(z, y, x, other)
    has_low, has_high = z > 0, z < planes - 1

    loads = [
        pltpu.make_async_copy(source, target, load_sem.at[index])
        for index, (source, target) in enumerate(
            ((emb_hbm, emb_ref), (bucket_hbm, bucket_ref), (valid_hbm, valid_ref))
        )
    ]
    for load in loads:
        load.start()

    barrier = pltpu.get_barrier_semaphore()

    def greet(device):
        pl.semaphore_signal(barrier, inc=1, device_id=device, device_id_type=pl.DeviceIdType.MESH)

    greet(partner)
    for spot in range(1, spots):
        greet(spot_device(spot))

    @pl.when(has_low)
    def _():
        greet(at(z - 1, y, x, core))

    @pl.when(has_high)
    def _():
        greet(at(z + 1, y, x, core))

    for load in loads:
        load.wait()
    floats = emb_ref[...].astype(jnp.float32)
    inverse = lax.rsqrt(jnp.mean(floats * floats, axis=1, keepdims=True) + 1e-06)
    unit = (floats * inverse).astype(jnp.bfloat16)
    keys[z, core] = unit
    queries[0] = unit
    meta = jnp.concatenate([bucket_ref[...], valid_ref[...]], axis=0).astype(jnp.float32)
    key_meta[z, core] = meta
    query_meta[0] = meta

    pl.semaphore_wait(barrier, jnp.where(has_low & has_high, spots + 2, spots + 1))

    def z_meta(source, way, to):
        ref = key_meta.at[source, core]
        return remote(
            ref, ref, zm_send.at[source, way], zm_recv.at[source], at(to, y, x, core)
        )

    def z_copy(source, way, to, part):
        ref = keys.at[source, core, pl.ds(part * piece, piece)]
        return remote(
            ref, ref, z_send.at[source, way, part], z_recv.at[source, part], at(to, y, x, core)
        )

    def c_meta(source, side):
        ref = key_meta.at[source, side]
        return remote(ref, ref, cm_send.at[source], cm_recv.at[source], partner)

    def c_copy(source, side, part):
        ref = keys.at[source, side, pl.ds(part * piece, piece)]
        return remote(ref, ref, c_send.at[source, part], c_recv.at[source, part], partner)

    def q_meta(spot):
        mine = seen_from(spot)
        return remote(
            query_meta.at[0], query_meta.at[mine], qm_send.at[spot], qm_recv.at[mine],
            spot_device(spot),
        )

    def q_copy(spot):
        mine = seen_from(spot)
        return remote(
            queries.at[0], queries.at[mine], q_send.at[spot], q_recv.at[mine], spot_device(spot)
        )

    def send_ways(source, act):
        @pl.when(has_high & ((source < z) | ((source == z) & (z < planes - 2))))
        def _():
            act(1, z + 1)

        @pl.when(has_low & ((source > z) | ((source == z) & (z > 1))))
        def _():
            act(0, z - 1)

    send_ways(z, lambda way, to: z_meta(z, way, to).start())
    for part in range(PIECES):
        send_ways(z, lambda way, to: z_copy(z, way, to, part).start())
    c_meta(z, core).start()
    for part in range(PIECES):
        c_copy(z, core, part).start()
    for spot in range(spots - 1, 0, -1):
        q_meta(spot).start()
        q_copy(spot).start()

    def column_of(spot):
        row = query_meta[spot, 0:1, :]
        query_col[spot] = jnp.transpose(jnp.broadcast_to(row, (rows, rows)))

    def terms(chosen, buckets, block, metas, own_keys):
        count = chosen.shape[0]
        cosine = lax.dot_general(
            chosen, block, (((1,), (1,)), ((), ())), preferred_element_type=jnp.float32
        ) * (1.0 / features)
        line = lax.broadcasted_iota(jnp.int32, (count, rows), 0)
        lane = lax.broadcasted_iota(jnp.int32, (count, rows), 1)
        factors = []
        peaks = None
        sums = None
        for index, (meta, own) in enumerate(zip(metas, own_keys)):
            wanted = jnp.where(meta[1:2, :] > 0, meta[0:1, :], -1.0)
            usable = buckets == wanted
            if own is not None:
                shift = jnp.where(own, 0, count + rows)
                usable = usable & (line + shift != lane)
            values = cosine[:, index * rows : (index + 1) * rows]
            best = jnp.where(usable, values, -1.0)
            factor = jnp.where(usable, jnp.exp(sharpness * (values - 1.0)), 0.0)
            factors.append(factor.astype(jnp.bfloat16))
            peaks = best if peaks is None else jnp.maximum(peaks, best)
            sums = factor if sums is None else sums + factor
        summed = jnp.dot(
            jnp.concatenate(factors, axis=1), block, preferred_element_type=jnp.float32
        )
        return peaks, sums, summed

    def absorb(first, last, source, fresh, sides=tuple(range(PAIR))):
        count = (last - first) * rows
        if len(sides) == PAIR:
            block = keys[source].reshape(PAIR * rows, features)
        else:
            block = keys[source, sides[0]]
        peaks, sums, summed = terms(
            queries[first:last].reshape(count, features),
            query_col[first:last].reshape(count, rows),
            block,
            [key_meta[source, side] for side in sides],
            [(source == z) & (core == side) if first == 0 else None for side in sides],
        )
        part = (last - first, rows)
        if fresh:
            peak[first:last] = peaks.reshape(*part, rows)
            weight[first:last] = sums.reshape(*part, rows)
            total[first:last] = summed.reshape(*part, features)
        else:
            peak[first:last] = jnp.maximum(peak[first:last], peaks.reshape(*part, rows))
            weight[first:last] += sums.reshape(*part, rows)
            total[first:last] += summed.reshape(*part, features)

    def wait_partner(source):
        c_meta(source, other).wait_recv()
        for part in range(PIECES):
            c_copy(source, other, part).wait_recv()

    def take(*arriving):
        for source in arriving:
            z_meta(source, 0, z).wait_recv()
            send_ways(source, lambda way, to: z_meta(source, way, to).start())
            c_meta(source, core).start()
        for part in range(PIECES):
            for source in arriving:
                z_copy(source, 0, z, part).wait_recv()
                send_ways(source, lambda way, to: z_copy(source, way, to, part).start())
                c_copy(source, core, part).start()

    orders = [arrival_order(place, planes) for place in range(planes)]

    def source_at(turn):
        source = jnp.int32(orders[0][turn])
        for place in range(1, planes):
            source = jnp.where(z == place, orders[place][turn], source)
        return source

    sources = [source_at(turn) for turn in range(planes - 1)]
    inner = has_low & has_high
    final = sources[-1]

    def at_end(source):
        @pl.when(jnp.logical_not(inner))
        def _():
            take(source)

    column_of(0)
    wait_partner(z)
    absorb(0, 1, z, True)

    @pl.when(inner)
    def _():
        take(*sources[:2])
        for source in sources[2:]:
            take(source)

    def each_source(act):
        for turn, source in enumerate(sources[:-1]):
            if turn == 1:

                @pl.when(inner)
                def _():
                    act(source)
            else:
                act(source)

    at_end(sources[0])
    for source in sources[2:-1]:
        at_end(source)

    def own_rows(source):
        wait_partner(source)
        absorb(0, 1, source, False)

    each_source(own_rows)

    def f_copies(spot):
        return (
            remote(
                query_meta.at[spot], plane_meta.at[spot], fm_send.at[spot], fm_recv.at[spot], partner
            ),
            remote(queries.at[spot], plane_keys.at[spot], f_send.at[spot], f_recv.at[spot], partner),
        )

    helper = (z == 1) | (z == planes - 2)
    end_z = jnp.where(z == 1, 0, planes - 1)

    for spot in range(1, spots):
        q_meta(seen_from(spot)).wait_recv()
        column_of(spot)
        q_copy(seen_from(spot)).wait_recv()

        @pl.when(helper)
        def _():
            for copy in f_copies(spot):
                copy.start()

    def h_copies():
        device = at(jnp.where(helper, end_z, z), y, x, core)
        return (
            remote(help_stat_out, help_stat_in, h_send.at[0], h_recv.at[0], device),
            remote(help_out, help_in, h_send.at[1], h_recv.at[1], device),
        )

    absorb(1, spots, z, True)

    @pl.when(helper)
    def _():
        row = key_meta[end_z, core, 0:1, :]
        column = jnp.transpose(jnp.broadcast_to(row, (rows, rows)))
        for spot in range(spots):
            if spot == 0:
                second, second_meta = keys[z, other], key_meta[z, other]
            else:
                for copy in f_copies(spot):
                    copy.wait_recv()
                second, second_meta = plane_keys[spot], plane_meta[spot]
            peaks, sums, summed = terms(
                keys[end_z, core],
                column,
                jnp.concatenate([queries[spot], second], axis=0),
                [query_meta[spot], second_meta],
                [None, None],
            )
            if spot == 0:
                help_peak[...] = peaks
                help_weight[...] = sums
                help_total[...] = summed
            else:
                help_peak[...] = jnp.maximum(help_peak[...], peaks)
                help_weight[...] += sums
                help_total[...] += summed
        help_out[...] = help_total[...].astype(jnp.bfloat16)
        top = jnp.max(jnp.transpose(help_peak[...]), axis=0, keepdims=True)
        mass = jnp.sum(jnp.transpose(help_weight[...]), axis=0, keepdims=True)
        help_stat_out[...] = jnp.concatenate([top, mass], axis=0)
        for copy in h_copies():
            copy.start()

    each_source(lambda source: absorb(1, spots, source, False))
    at_end(final)
    absorb(1, spots, final, False, (core,))
    wait_partner(final)

    def stat_rows(spot):
        top = jnp.max(jnp.transpose(peak[spot]), axis=0, keepdims=True)
        mass = jnp.sum(jnp.transpose(weight[spot]), axis=0, keepdims=True)
        return top, mass

    across, along = columns, 1
    corner = across + along
    half = rows // 2
    halves = (pl.ds(0, half), pl.ds(half, half))

    def p_copy(spot, side):
        mine = seen_from(spot)
        return remote(
            part_out.at[spot, halves[side]], part_in.at[mine, halves[side]],
            p_send.at[spot, side], p_recv.at[mine, side], spot_device(spot),
        )

    def corner_copy(side):
        spot = (along, across)[side]
        return remote(
            part_out.at[corner, halves[side]], part_in.at[corner, halves[side]],
            p_send.at[corner, side], p_recv.at[corner, side], spot_device(spot),
        )

    def s_copy(spot):
        mine = seen_from(spot)
        return remote(
            stat_out.at[spot], stat_in.at[mine], s_send.at[spot], s_recv.at[mine],
            spot_device(spot),
        )

    absorb(corner, corner + 1, final, False, (other,))
    part_out[corner] = total[corner].astype(jnp.bfloat16)
    corner_copy(0).start()
    corner_copy(1).start()
    passing = ((along, 1), (across, 0))
    for spot, side in passing:
        absorb(spot, spot + 1, final, False, (other,))
        part_out[spot, halves[1 - side]] = total[spot, halves[1 - side]].astype(jnp.bfloat16)
        p_copy(spot, 1 - side).start()
    for spot in range(spots - 1, 0, -1):
        stat_out[spot] = jnp.concatenate(stat_rows(spot), axis=0)
        s_copy(spot).start()
    absorb(0, 1, final, False)
    stat_in[0] = jnp.concatenate(stat_rows(0), axis=0)
    total[0] += queries[0].astype(jnp.float32)
    for spot, side in passing:
        corner_copy(side).wait_recv()
        part_out[spot, halves[side]] = (
            total[spot, halves[side]] + part_in[corner, halves[side]].astype(jnp.float32)
        ).astype(jnp.bfloat16)
        p_copy(spot, side).start()

    @pl.when(jnp.logical_not(inner))
    def _():
        for copy in h_copies():
            copy.wait_recv()
        stat_in[0] = jnp.concatenate(
            [
                jnp.maximum(stat_in[0, 0:1, :], help_stat_in[0:1, :]),
                stat_in[0, 1:2, :] + help_stat_in[1:2, :],
            ],
            axis=0,
        )
        total[0] += help_in[...].astype(jnp.float32)

    top, mass = stat_in[0, 0:1, :], stat_in[0, 1:2, :]
    for spot in range(1, spots):
        s_copy(seen_from(spot)).wait_recv()
        top = jnp.maximum(top, stat_in[spot, 0:1, :])
        mass = mass + stat_in[spot, 1:2, :]
    best_ref[...] = top.astype(jnp.bfloat16)
    below = jnp.transpose(jnp.broadcast_to(1.0 + mass, (rows, rows)))[:, 0:1]
    for spot, _ in passing:
        for side in range(2):
            p_copy(seen_from(spot), side).wait_recv()
    result = total[0]
    for spot, _ in passing:
        result = result + part_in[spot].astype(jnp.float32)
    mean_ref[...] = (result / below).astype(jnp.bfloat16)

    send_ways(z, lambda way, to: z_meta(z, way, to).wait_send())
    for part in range(PIECES):
        send_ways(z, lambda way, to: z_copy(z, way, to, part).wait_send())
    c_meta(z, core).wait_send()
    for part in range(PIECES):
        c_copy(z, core, part).wait_send()
    def sent(source):
        send_ways(source, lambda way, to: z_meta(source, way, to).wait_send())
        c_meta(source, core).wait_send()
        for part in range(PIECES):
            send_ways(source, lambda way, to: z_copy(source, way, to, part).wait_send())
            c_copy(source, core, part).wait_send()

    each_source(sent)
    sent(final)

    @pl.when(helper)
    def _():
        for spot in range(1, spots):
            for copy in f_copies(spot):
                copy.wait_send()
        for copy in h_copies():
            copy.wait_send()

    for spot in range(1, spots):
        q_meta(spot).wait_send()
        q_copy(spot).wait_send()
        s_copy(spot).wait_send()
    for side in range(2):
        corner_copy(side).wait_send()
        for spot, _ in passing:
            p_copy(spot, side).wait_send()


def dense(embeddings, bucket_ids, valid_rows):
    rows, features = embeddings.shape
    planes = lax.axis_size("wide") // PAIR
    spots = lax.axis_size("blk")
    dma = pltpu.SemaphoreType.DMA
    vmem = pl.BlockSpec(memory_space=pltpu.VMEM)
    mean, best = pl.pallas_call(
        functools.partial(dense_kernel, planes),
        out_shape=(
            jax.ShapeDtypeStruct((rows, features), jnp.bfloat16),
            jax.ShapeDtypeStruct((1, rows), jnp.bfloat16),
        ),
        in_specs=[pl.BlockSpec(memory_space=pltpu.HBM)] * 3,
        out_specs=(vmem, vmem),
        scratch_shapes=[
            pltpu.VMEM((rows, features), jnp.bfloat16),
            pltpu.VMEM((1, rows), jnp.int32),
            pltpu.VMEM((1, rows), jnp.int32),
            dma((3,)),
            pltpu.VMEM((planes, PAIR, rows, features), jnp.bfloat16),
            pltpu.VMEM((planes, PAIR, 2, rows), jnp.float32),
            pltpu.VMEM((spots, rows, features), jnp.bfloat16),
            pltpu.VMEM((spots, 2, rows), jnp.float32),
            pltpu.VMEM((spots, rows, rows), jnp.float32),
            pltpu.VMEM((spots, rows, features), jnp.float32),
            pltpu.VMEM((spots, rows, rows), jnp.float32),
            pltpu.VMEM((spots, rows, rows), jnp.float32),
            pltpu.VMEM((spots, rows, features), jnp.bfloat16),
            pltpu.VMEM((spots, rows, features), jnp.bfloat16),
            pltpu.VMEM((spots, 2, rows), jnp.float32),
            pltpu.VMEM((spots, 2, rows), jnp.float32),
            pltpu.VMEM((spots, rows, features), jnp.bfloat16),
            pltpu.VMEM((spots, 2, rows), jnp.float32),
            pltpu.VMEM((rows, features), jnp.float32),
            pltpu.VMEM((rows, rows), jnp.float32),
            pltpu.VMEM((rows, rows), jnp.float32),
            pltpu.VMEM((rows, features), jnp.bfloat16),
            pltpu.VMEM((rows, features), jnp.bfloat16),
            pltpu.VMEM((2, rows), jnp.float32),
            pltpu.VMEM((2, rows), jnp.float32),
            dma((planes, 2, PIECES)), dma((planes, PIECES)), dma((planes, 2)), dma((planes,)),
            dma((planes, PIECES)), dma((planes, PIECES)), dma((planes,)), dma((planes,)),
            dma((spots,)), dma((spots,)), dma((spots,)), dma((spots,)),
            dma((spots, 2)), dma((spots, 2)), dma((spots,)), dma((spots,)),
            dma((spots,)), dma((spots,)), dma((spots,)), dma((spots,)), dma((2,)), dma((2,)),
        ],
        compiler_params=pltpu.CompilerParams(
            collective_id=0, has_side_effects=True, vmem_limit_bytes=GRANT
        ),
    )(embeddings, bucket_ids.reshape(1, rows), valid_rows.reshape(1, rows))
    return mean, best.reshape(rows)


def on_device(embeddings, bucket_ids, slot_ids, valid_rows):
    rows = embeddings.shape[0]
    groups = lax.axis_size("wide")
    blocks = lax.axis_size("blk")
    bucket_work = blocks * (2 * rows) ** 2
    dense_work = groups * blocks * rows**2
    fits = groups % PAIR == 0 and groups >= 4 * PAIR and blocks == PAIR * PAIR and rows == 128
    if fits and dense_work <= 4 * bucket_work:
        return dense(embeddings, bucket_ids, valid_rows)
    return by_bucket(embeddings, bucket_ids, slot_ids, valid_rows)


def solution(mesh):
    in_specs = (
        P(("wide", "blk"), None),
        P(("wide", "blk")),
        P(("wide", "blk")),
        P(("wide", "blk")),
    )
    out_specs = (P(("wide", "blk"), None), P(("wide", "blk")))
    return jax.shard_map(
        on_device, mesh=mesh, in_specs=in_specs, out_specs=out_specs, check_vma=False
    )
```

```python
import functools

import jax
import jax.numpy as jnp
from jax import lax
from jax.experimental import pallas as pl
from jax.experimental.pallas import tpu as pltpu
from jax.sharding import PartitionSpec as P

sharpness = 10.0


def from_behind(value, axis, steps):
    count = lax.axis_size(axis)
    pairs = [(source, (source + steps) % count) for source in range(count)]
    return lax.ppermute(value, axis, pairs)


def unit_rows(embeddings):
    float_rows = embeddings.astype(jnp.float32)
    inverse_norm = lax.rsqrt(jnp.mean(float_rows * float_rows, axis=1, keepdims=True) + 1e-06)
    return (float_rows * inverse_norm).astype(jnp.bfloat16)


def bucket_stats(queries, query_pos, key_rows, key_flags, key_pos):
    feature_count = queries.shape[1]
    cosine = (
        lax.dot_general(
            queries, key_rows, (((1,), (1,)), ((), ())), preferred_element_type=jnp.float32
        )
        / feature_count
    )
    usable = (key_flags[None, :] > 0) & (query_pos[:, None] != key_pos[None, :])
    best_cos = jnp.max(jnp.where(usable, cosine, -1.0), axis=1)
    weights = jnp.where(usable, jnp.exp(sharpness * (cosine - 1.0)), 0.0)
    weight_total = jnp.sum(weights, axis=1)
    summed = jnp.dot(weights.astype(jnp.bfloat16), key_rows, preferred_element_type=jnp.float32)
    return (best_cos, weight_total, summed)


def by_bucket(embeddings, bucket_ids, slot_ids, valid_rows):
    unit_vectors = unit_rows(embeddings)
    row_count, feature_count = unit_vectors.shape
    groups = lax.axis_size("wide")
    blocks = lax.axis_size("blk")
    slot_count = 2 * row_count // groups
    block_rows = groups * slot_count
    cell_ids = bucket_ids * slot_count + slot_ids
    outgoing = jnp.zeros((block_rows, feature_count), jnp.bfloat16).at[cell_ids].set(unit_vectors)
    flag_rows = (
        jnp.zeros((block_rows,), jnp.bfloat16).at[cell_ids].set(valid_rows.astype(jnp.bfloat16))
    )
    arrived, arrived_flags = (
        lax.all_to_all(
            outgoing.reshape(groups, slot_count, feature_count),
            "wide",
            split_axis=0,
            concat_axis=0,
            tiled=True,
        ),
        lax.all_to_all(
            flag_rows.reshape(groups, slot_count), "wide", split_axis=0, concat_axis=0, tiled=True
        ),
    )
    queries = arrived.reshape(block_rows, feature_count)
    query_flags = arrived_flags.reshape(block_rows)
    my_block = lax.axis_index("blk")
    query_pos = my_block * block_rows + jnp.arange(block_rows, dtype=jnp.int32)

    def absorb(running, key_rows, key_flags, key_start):
        key_pos = key_start + jnp.arange(key_rows.shape[0], dtype=jnp.int32)
        best_cos, weight_total, summed = bucket_stats(
            queries, query_pos, key_rows, key_flags, key_pos
        )
        return (jnp.maximum(running[0], best_cos), running[1] + weight_total, running[2] + summed)

    initial = (
        jnp.full((block_rows,), -1.0, jnp.float32),
        jnp.zeros((block_rows,), jnp.float32),
        jnp.zeros((block_rows, feature_count), jnp.float32),
    )
    key_rows, key_flags = (queries, query_flags)
    running = absorb(initial, key_rows, key_flags, my_block * block_rows)
    for turn_index in range(1, blocks):
        key_rows, key_flags = from_behind((key_rows, key_flags), "blk", 1)
        running = absorb(
            running, key_rows, key_flags, (my_block - turn_index) % blocks * block_rows
        )
    best_cos, weight_total, summed = running
    mean_rows = ((queries.astype(jnp.float32) + summed) / (1.0 + weight_total[:, None])).astype(
        jnp.bfloat16
    )
    back_mean, back_best = (
        lax.all_to_all(
            mean_rows.reshape(groups, slot_count, feature_count),
            "wide",
            split_axis=0,
            concat_axis=0,
            tiled=True,
        ),
        lax.all_to_all(
            best_cos.astype(jnp.bfloat16).reshape(groups, slot_count),
            "wide",
            split_axis=0,
            concat_axis=0,
            tiled=True,
        ),
    )
    neighbour_mean = back_mean.reshape(block_rows, feature_count)[cell_ids]
    max_cosine = back_best.reshape(block_rows)[cell_ids]
    return (neighbour_mean, max_cosine)


PAIR = 2
PIECES = 4
GRANT = 56_240_000


def arrival_order(place, count):
    low, high = place, count - 1 - place
    order = []
    for distance in range(1, count):
        if distance <= low:
            order.append(place - distance)
        if distance <= high:
            order.append(place + distance)
    if low == 0 or high == 0:
        order = [order[1], order[1]] + order[2:]
    return order


def dense_kernel(
    planes, emb_hbm, bucket_hbm, valid_hbm, mean_ref, best_ref,
    emb_ref, bucket_ref, valid_ref, load_sem,
    keys, key_meta, queries, query_meta, query_col, total, peak, weight,
    part_out, part_in, stat_out, stat_in,
    plane_keys, plane_meta, help_total, help_peak, help_weight,
    help_out, help_in, help_stat_out, help_stat_in,
    z_send, z_recv, zm_send, zm_recv, c_send, c_recv, cm_send, cm_recv,
    q_send, q_recv, qm_send, qm_recv, p_send, p_recv, s_send, s_recv,
    f_send, f_recv, fm_send, fm_recv, h_send, h_recv,
):
    rows, features = emb_ref.shape
    spots = queries.shape[0]
    wide, blk = lax.axis_index("wide"), lax.axis_index("blk")
    z, y = lax.div(wide, PAIR), lax.rem(wide, PAIR)
    x, core = lax.div(blk, PAIR), lax.rem(blk, PAIR)
    other = 1 - core
    columns = spots // PAIR
    piece = rows // PIECES

    def at(z_at, y_at, x_at, core_at):
        return (z_at * PAIR + y_at, x_at * PAIR + core_at)

    def spot_device(spot):
        dy, dx = divmod(spot, columns)
        return at(z, lax.rem(y + dy, PAIR), lax.rem(x + dx, columns), core)

    def seen_from(spot):
        dy, dx = divmod(spot, columns)
        return (-dy) % PAIR * columns + (-dx) % columns

    def remote(source, target, send, recv, device):
        return pltpu.make_async_remote_copy(
            src_ref=source, dst_ref=target, send_sem=send, recv_sem=recv,
            device_id=device, device_id_type=pl.DeviceIdType.MESH,
        )

    partner = at(z, y, x, other)
    has_low, has_high = z > 0, z < planes - 1

    loads = [
        pltpu.make_async_copy(source, target, load_sem.at[index])
        for index, (source, target) in enumerate(
            ((emb_hbm, emb_ref), (bucket_hbm, bucket_ref), (valid_hbm, valid_ref))
        )
    ]
    for load in loads:
        load.start()

    barrier = pltpu.get_barrier_semaphore()

    def greet(device):
        pl.semaphore_signal(barrier, inc=1, device_id=device, device_id_type=pl.DeviceIdType.MESH)

    greet(partner)
    for spot in range(1, spots):
        greet(spot_device(spot))

    @pl.when(has_low)
    def _():
        greet(at(z - 1, y, x, core))

    @pl.when(has_high)
    def _():
        greet(at(z + 1, y, x, core))

    for load in loads:
        load.wait()
    floats = emb_ref[...].astype(jnp.float32)
    inverse = lax.rsqrt(jnp.mean(floats * floats, axis=1, keepdims=True) + 1e-06)
    unit = (floats * inverse).astype(jnp.bfloat16)
    keys[z, core] = unit
    queries[0] = unit
    meta = jnp.concatenate([bucket_ref[...], valid_ref[...]], axis=0).astype(jnp.float32)
    key_meta[z, core] = meta
    query_meta[0] = meta

    pl.semaphore_wait(barrier, jnp.where(has_low & has_high, spots + 2, spots + 1))

    def z_meta(source, way, to):
        ref = key_meta.at[source, core]
        return remote(
            ref, ref, zm_send.at[source, way], zm_recv.at[source], at(to, y, x, core)
        )

    def z_copy(source, way, to, part):
        ref = keys.at[source, core, pl.ds(part * piece, piece)]
        return remote(
            ref, ref, z_send.at[source, way, part], z_recv.at[source, part], at(to, y, x, core)
        )

    def c_meta(source, side):
        ref = key_meta.at[source, side]
        return remote(ref, ref, cm_send.at[source], cm_recv.at[source], partner)

    def c_copy(source, side, part):
        ref = keys.at[source, side, pl.ds(part * piece, piece)]
        return remote(ref, ref, c_send.at[source, part], c_recv.at[source, part], partner)

    def q_meta(spot):
        mine = seen_from(spot)
        return remote(
            query_meta.at[0], query_meta.at[mine], qm_send.at[spot], qm_recv.at[mine],
            spot_device(spot),
        )

    def q_copy(spot):
        mine = seen_from(spot)
        return remote(
            queries.at[0], queries.at[mine], q_send.at[spot], q_recv.at[mine], spot_device(spot)
        )

    def send_ways(source, act):
        @pl.when(has_high & ((source < z) | ((source == z) & (z < planes - 2))))
        def _():
            act(1, z + 1)

        @pl.when(has_low & ((source > z) | ((source == z) & (z > 1))))
        def _():
            act(0, z - 1)

    send_ways(z, lambda way, to: z_meta(z, way, to).start())
    for part in range(PIECES):
        send_ways(z, lambda way, to: z_copy(z, way, to, part).start())
    c_meta(z, core).start()
    for part in range(PIECES):
        c_copy(z, core, part).start()
    for spot in range(spots - 1, 0, -1):
        q_meta(spot).start()
        q_copy(spot).start()

    def column_of(spot):
        row = query_meta[spot, 0:1, :]
        query_col[spot] = jnp.transpose(jnp.broadcast_to(row, (rows, rows)))

    def terms(chosen, buckets, block, metas, own_keys):
        count = chosen.shape[0]
        cosine = lax.dot_general(
            chosen, block, (((1,), (1,)), ((), ())), preferred_element_type=jnp.float32
        ) * (1.0 / features)
        line = lax.broadcasted_iota(jnp.int32, (count, rows), 0)
        lane = lax.broadcasted_iota(jnp.int32, (count, rows), 1)
        factors = []
        peaks = None
        sums = None
        for index, (meta, own) in enumerate(zip(metas, own_keys)):
            wanted = jnp.where(meta[1:2, :] > 0, meta[0:1, :], -1.0)
            usable = buckets == wanted
            if own is not None:
                shift = jnp.where(own, 0, count + rows)
                usable = usable & (line + shift != lane)
            values = cosine[:, index * rows : (index + 1) * rows]
            best = jnp.where(usable, values, -1.0)
            factor = jnp.where(usable, jnp.exp(sharpness * (values - 1.0)), 0.0)
            factors.append(factor.astype(jnp.bfloat16))
            peaks = best if peaks is None else jnp.maximum(peaks, best)
            sums = factor if sums is None else sums + factor
        summed = jnp.dot(
            jnp.concatenate(factors, axis=1), block, preferred_element_type=jnp.float32
        )
        return peaks, sums, summed

    def absorb(first, last, source, fresh, sides=tuple(range(PAIR))):
        count = (last - first) * rows
        if len(sides) == PAIR:
            block = keys[source].reshape(PAIR * rows, features)
        else:
            block = keys[source, sides[0]]
        peaks, sums, summed = terms(
            queries[first:last].reshape(count, features),
            query_col[first:last].reshape(count, rows),
            block,
            [key_meta[source, side] for side in sides],
            [(source == z) & (core == side) if first == 0 else None for side in sides],
        )
        part = (last - first, rows)
        if fresh:
            peak[first:last] = peaks.reshape(*part, rows)
            weight[first:last] = sums.reshape(*part, rows)
            total[first:last] = summed.reshape(*part, features)
        else:
            peak[first:last] = jnp.maximum(peak[first:last], peaks.reshape(*part, rows))
            weight[first:last] += sums.reshape(*part, rows)
            total[first:last] += summed.reshape(*part, features)

    def wait_partner(source):
        c_meta(source, other).wait_recv()
        for part in range(PIECES):
            c_copy(source, other, part).wait_recv()

    def take(*arriving):
        for source in arriving:
            z_meta(source, 0, z).wait_recv()
            send_ways(source, lambda way, to: z_meta(source, way, to).start())
            c_meta(source, core).start()
        for part in range(PIECES):
            for source in arriving:
                z_copy(source, 0, z, part).wait_recv()
                send_ways(source, lambda way, to: z_copy(source, way, to, part).start())
                c_copy(source, core, part).start()

    orders = [arrival_order(place, planes) for place in range(planes)]

    def source_at(turn):
        source = jnp.int32(orders[0][turn])
        for place in range(1, planes):
            source = jnp.where(z == place, orders[place][turn], source)
        return source

    sources = [source_at(turn) for turn in range(planes - 1)]
    inner = has_low & has_high
    final = sources[-1]

    def at_end(source):
        @pl.when(jnp.logical_not(inner))
        def _():
            take(source)

    column_of(0)
    wait_partner(z)
    absorb(0, 1, z, True)

    @pl.when(inner)
    def _():
        take(*sources[:2])
        for source in sources[2:]:
            take(source)

    def each_source(act):
        for turn, source in enumerate(sources[:-1]):
            if turn == 1:

                @pl.when(inner)
                def _():
                    act(source)
            else:
                act(source)

    at_end(sources[0])
    for source in sources[2:-1]:
        at_end(source)

    def own_rows(source):
        wait_partner(source)
        absorb(0, 1, source, False)

    each_source(own_rows)

    def f_copies(spot):
        return (
            remote(
                query_meta.at[spot], plane_meta.at[spot], fm_send.at[spot], fm_recv.at[spot], partner
            ),
            remote(queries.at[spot], plane_keys.at[spot], f_send.at[spot], f_recv.at[spot], partner),
        )

    helper = (z == 1) | (z == planes - 2)
    end_z = jnp.where(z == 1, 0, planes - 1)

    for spot in range(1, spots):
        q_meta(seen_from(spot)).wait_recv()
        column_of(spot)
        q_copy(seen_from(spot)).wait_recv()

        @pl.when(helper)
        def _():
            for copy in f_copies(spot):
                copy.start()

    def h_copies():
        device = at(jnp.where(helper, end_z, z), y, x, core)
        return (
            remote(help_stat_out, help_stat_in, h_send.at[0], h_recv.at[0], device),
            remote(help_out, help_in, h_send.at[1], h_recv.at[1], device),
        )

    absorb(1, spots, z, True)

    each_source(lambda source: absorb(1, spots, source, False))
    at_end(final)
    absorb(1, spots, final, False, (core,))
    wait_partner(final)

    def stat_rows(spot):
        top = jnp.max(jnp.transpose(peak[spot]), axis=0, keepdims=True)
        mass = jnp.sum(jnp.transpose(weight[spot]), axis=0, keepdims=True)
        return top, mass

    across, along = columns, 1
    corner = across + along
    half = rows // 2
    halves = (pl.ds(0, half), pl.ds(half, half))

    def p_copy(spot, side):
        mine = seen_from(spot)
        return remote(
            part_out.at[spot, halves[side]], part_in.at[mine, halves[side]],
            p_send.at[spot, side], p_recv.at[mine, side], spot_device(spot),
        )

    def corner_copy(side):
        spot = (along, across)[side]
        return remote(
            part_out.at[corner, halves[side]], part_in.at[corner, halves[side]],
            p_send.at[corner, side], p_recv.at[corner, side], spot_device(spot),
        )

    def s_copy(spot):
        mine = seen_from(spot)
        return remote(
            stat_out.at[spot], stat_in.at[mine], s_send.at[spot], s_recv.at[mine],
            spot_device(spot),
        )

    absorb(corner, corner + 1, final, False, (other,))
    part_out[corner] = total[corner].astype(jnp.bfloat16)
    corner_copy(0).start()
    corner_copy(1).start()
    passing = ((along, 1), (across, 0))
    for spot, side in passing:
        absorb(spot, spot + 1, final, False, (other,))
        part_out[spot, halves[1 - side]] = total[spot, halves[1 - side]].astype(jnp.bfloat16)
        p_copy(spot, 1 - side).start()
    for spot in range(spots - 1, 0, -1):
        stat_out[spot] = jnp.concatenate(stat_rows(spot), axis=0)
        s_copy(spot).start()
    @pl.when(helper)
    def _():
        row = key_meta[end_z, core, 0:1, :]
        column = jnp.transpose(jnp.broadcast_to(row, (rows, rows)))
        for spot in range(spots):
            if spot == 0:
                second, second_meta = keys[z, other], key_meta[z, other]
            else:
                for copy in f_copies(spot):
                    copy.wait_recv()
                second, second_meta = plane_keys[spot], plane_meta[spot]
            peaks, sums, summed = terms(
                keys[end_z, core],
                column,
                jnp.concatenate([queries[spot], second], axis=0),
                [query_meta[spot], second_meta],
                [None, None],
            )
            if spot == 0:
                help_peak[...] = peaks
                help_weight[...] = sums
                help_total[...] = summed
            else:
                help_peak[...] = jnp.maximum(help_peak[...], peaks)
                help_weight[...] += sums
                help_total[...] += summed
        help_out[...] = help_total[...].astype(jnp.bfloat16)
        top = jnp.max(jnp.transpose(help_peak[...]), axis=0, keepdims=True)
        mass = jnp.sum(jnp.transpose(help_weight[...]), axis=0, keepdims=True)
        help_stat_out[...] = jnp.concatenate([top, mass], axis=0)
        for copy in h_copies():
            copy.start()

    for spot, side in passing:
        corner_copy(side).wait_recv()
        part_out[spot, halves[side]] = (
            total[spot, halves[side]] + part_in[corner, halves[side]].astype(jnp.float32)
        ).astype(jnp.bfloat16)
        p_copy(spot, side).start()

    absorb(0, 1, final, False)
    stat_in[0] = jnp.concatenate(stat_rows(0), axis=0)
    total[0] += queries[0].astype(jnp.float32)

    @pl.when(jnp.logical_not(inner))
    def _():
        for copy in h_copies():
            copy.wait_recv()
        stat_in[0] = jnp.concatenate(
            [
                jnp.maximum(stat_in[0, 0:1, :], help_stat_in[0:1, :]),
                stat_in[0, 1:2, :] + help_stat_in[1:2, :],
            ],
            axis=0,
        )
        total[0] += help_in[...].astype(jnp.float32)

    top, mass = stat_in[0, 0:1, :], stat_in[0, 1:2, :]
    for spot in range(1, spots):
        s_copy(seen_from(spot)).wait_recv()
        top = jnp.maximum(top, stat_in[spot, 0:1, :])
        mass = mass + stat_in[spot, 1:2, :]
    best_ref[...] = top.astype(jnp.bfloat16)
    below = jnp.transpose(jnp.broadcast_to(1.0 + mass, (rows, rows)))[:, 0:1]
    for spot, _ in passing:
        for side in range(2):
            p_copy(seen_from(spot), side).wait_recv()
    result = total[0]
    for spot, _ in passing:
        result = result + part_in[spot].astype(jnp.float32)
    mean_ref[...] = (result / below).astype(jnp.bfloat16)

    send_ways(z, lambda way, to: z_meta(z, way, to).wait_send())
    for part in range(PIECES):
        send_ways(z, lambda way, to: z_copy(z, way, to, part).wait_send())
    c_meta(z, core).wait_send()
    for part in range(PIECES):
        c_copy(z, core, part).wait_send()
    def sent(source):
        send_ways(source, lambda way, to: z_meta(source, way, to).wait_send())
        c_meta(source, core).wait_send()
        for part in range(PIECES):
            send_ways(source, lambda way, to: z_copy(source, way, to, part).wait_send())
            c_copy(source, core, part).wait_send()

    each_source(sent)
    sent(final)

    @pl.when(helper)
    def _():
        for spot in range(1, spots):
            for copy in f_copies(spot):
                copy.wait_send()
        for copy in h_copies():
            copy.wait_send()

    for spot in range(1, spots):
        q_meta(spot).wait_send()
        q_copy(spot).wait_send()
        s_copy(spot).wait_send()
    for side in range(2):
        corner_copy(side).wait_send()
        for spot, _ in passing:
            p_copy(spot, side).wait_send()


def dense(embeddings, bucket_ids, valid_rows):
    rows, features = embeddings.shape
    planes = lax.axis_size("wide") // PAIR
    spots = lax.axis_size("blk")
    dma = pltpu.SemaphoreType.DMA
    vmem = pl.BlockSpec(memory_space=pltpu.VMEM)
    mean, best = pl.pallas_call(
        functools.partial(dense_kernel, planes),
        out_shape=(
            jax.ShapeDtypeStruct((rows, features), jnp.bfloat16),
            jax.ShapeDtypeStruct((1, rows), jnp.bfloat16),
        ),
        in_specs=[pl.BlockSpec(memory_space=pltpu.HBM)] * 3,
        out_specs=(vmem, vmem),
        scratch_shapes=[
            pltpu.VMEM((rows, features), jnp.bfloat16),
            pltpu.VMEM((1, rows), jnp.int32),
            pltpu.VMEM((1, rows), jnp.int32),
            dma((3,)),
            pltpu.VMEM((planes, PAIR, rows, features), jnp.bfloat16),
            pltpu.VMEM((planes, PAIR, 2, rows), jnp.float32),
            pltpu.VMEM((spots, rows, features), jnp.bfloat16),
            pltpu.VMEM((spots, 2, rows), jnp.float32),
            pltpu.VMEM((spots, rows, rows), jnp.float32),
            pltpu.VMEM((spots, rows, features), jnp.float32),
            pltpu.VMEM((spots, rows, rows), jnp.float32),
            pltpu.VMEM((spots, rows, rows), jnp.float32),
            pltpu.VMEM((spots, rows, features), jnp.bfloat16),
            pltpu.VMEM((spots, rows, features), jnp.bfloat16),
            pltpu.VMEM((spots, 2, rows), jnp.float32),
            pltpu.VMEM((spots, 2, rows), jnp.float32),
            pltpu.VMEM((spots, rows, features), jnp.bfloat16),
            pltpu.VMEM((spots, 2, rows), jnp.float32),
            pltpu.VMEM((rows, features), jnp.float32),
            pltpu.VMEM((rows, rows), jnp.float32),
            pltpu.VMEM((rows, rows), jnp.float32),
            pltpu.VMEM((rows, features), jnp.bfloat16),
            pltpu.VMEM((rows, features), jnp.bfloat16),
            pltpu.VMEM((2, rows), jnp.float32),
            pltpu.VMEM((2, rows), jnp.float32),
            dma((planes, 2, PIECES)), dma((planes, PIECES)), dma((planes, 2)), dma((planes,)),
            dma((planes, PIECES)), dma((planes, PIECES)), dma((planes,)), dma((planes,)),
            dma((spots,)), dma((spots,)), dma((spots,)), dma((spots,)),
            dma((spots, 2)), dma((spots, 2)), dma((spots,)), dma((spots,)),
            dma((spots,)), dma((spots,)), dma((spots,)), dma((spots,)), dma((2,)), dma((2,)),
        ],
        compiler_params=pltpu.CompilerParams(
            collective_id=0, has_side_effects=True, vmem_limit_bytes=GRANT
        ),
    )(embeddings, bucket_ids.reshape(1, rows), valid_rows.reshape(1, rows))
    return mean, best.reshape(rows)


def on_device(embeddings, bucket_ids, slot_ids, valid_rows):
    rows = embeddings.shape[0]
    groups = lax.axis_size("wide")
    blocks = lax.axis_size("blk")
    bucket_work = blocks * (2 * rows) ** 2
    dense_work = groups * blocks * rows**2
    fits = groups % PAIR == 0 and groups >= 4 * PAIR and blocks == PAIR * PAIR and rows == 128
    if fits and dense_work <= 4 * bucket_work:
        return dense(embeddings, bucket_ids, valid_rows)
    return by_bucket(embeddings, bucket_ids, slot_ids, valid_rows)


def solution(mesh):
    in_specs = (
        P(("wide", "blk"), None),
        P(("wide", "blk")),
        P(("wide", "blk")),
        P(("wide", "blk")),
    )
    out_specs = (P(("wide", "blk"), None), P(("wide", "blk")))
    return jax.shard_map(
        on_device, mesh=mesh, in_specs=in_specs, out_specs=out_specs, check_vma=False
    )
```
